512 devices in a mesh: aux: 32 (over y, x), ao: 16 (over z, core).
Axes of the slice: x: 4, y: 8, z: 8, core: 2. Of those that a mesh axis runs over, the one named last changes fastest.
Arguments:
- tile_values: bfloat16 [8192, 48, 2304], P(('aux', 'ao')), may hold values from -6 to 6
- tile_owner: int32 [8192, 1], P(('aux', 'ao')), may hold values from 0 to 15; in each aligned block of 16 rows (0 to 15, 16 to 31, ...) at most 2 rows name the same one
- tile_block: int32 [8192], P(('aux', 'ao')), may hold values from 0 to 7
- coefficients: bfloat16 [128, 48, 512], P('ao'), may hold values from -0.21875 to 0.21875
Outputs:
- exchange_band: float32 [16, 3840], P('ao', 'aux')
The draws below stay inside these ranges and needn't reach their ends.
Inputs may be any that keep to these rules, and one draw needn't show every extreme that they name: `tile_owner`: among the 16 tiles of one device at most 2 name the same ao index, and in some device exactly 2 do.
All inputs are finite; a program needn't handle non-finite values.
Results may differ from the reference program's by a relative error of at most 0.004.
Values may be sent and summed in bfloat16 or wider, within the bound.
A program may use at most 64 MiB of HBM per device.

```python
import math
import jax
import jax.numpy as jnp
import numpy as np
from jax import lax

BS = 48
HW = 16
TILES_DEV = 16
LB_DEV = 8
NOCC = 256
CAP = 2
TILES = 8192
NLAM = 128
N_AUX = 32
N_AO = 16


def place_ends(entries, rng, low, largest):
    index_at = [jax.random.randint(jax.random.fold_in(rng, axis), (), 0, length) for axis, length in enumerate(entries.shape)]
    widest = entries.shape.index(max(entries.shape))
    beside = index_at[:widest] + [(index_at[widest] + 1) % entries.shape[widest]] + index_at[widest + 1:]
    return entries.at[tuple(index_at)].set(low).at[tuple(beside)].set(largest)


def block_levels(stream_key, dims, split, low, largest):
    gain = 1.0
    for dim, parts in split:
        heights = jax.random.uniform(jax.random.fold_in(jax.random.fold_in(stream_key, 6), dim), (parts,), jnp.float32, low / len(split), largest / len(split))
        gain = gain * jnp.repeat(jnp.exp(heights), dims[dim] // parts).reshape((-1,) + (1,) * (len(dims) - 1 - dim))
    return gain


def routed_block(key, own, number, rows, amount, top, bound, skew):
    order = jax.random.permutation(key, amount)
    crowded, ordinary = shares(amount, rows * top, bound, skew, True), shares(amount, rows * top, bound, skew, False)
    places = jnp.arange(amount)

    def named(sizes, offset_by):
        used = int((sizes > 0).sum())
        fixed = max(1, used // 4)
        passed = fixed + (places - fixed + offset_by * (used - fixed)) % max(1, amount - fixed)
        return jnp.zeros((amount,), jnp.int32).at[order[jnp.where(places < fixed, places, passed)]].set(jnp.asarray(sizes, jnp.int32))

    sizes = jnp.where(number % 4 == 0, named(crowded, number // 4), named(ordinary, number - number // 4 - 1))
    mixed = jax.random.permutation(jax.random.fold_in(own, 3), amount)
    giver, receiver = mixed[0:amount // 2 * 2:2], mixed[1:amount // 2 * 2:2]
    slack = jnp.minimum(sizes[giver] - 1, bound - sizes[receiver]) // 2
    slack = jnp.where((giver == order[0]) | (receiver == order[0]) | (sizes[receiver] == 0), 0, jnp.maximum(slack, 0))
    passed = jax.random.randint(jax.random.fold_in(own, 4), (amount // 2,), 0, 1 << 20) % (slack + 1)
    sizes = sizes.at[giver].add(-passed).at[receiver].add(passed)
    members = jnp.searchsorted(jnp.cumsum(sizes), jnp.arange(rows * top), side="right").astype(jnp.int32)
    table = members.reshape(top, rows).T
    table = table[jax.random.permutation(jax.random.fold_in(own, 1), rows)]
    offset_by = jax.random.randint(jax.random.fold_in(own, 2), (rows, 1), 0, top)
    return jnp.take_along_axis(table, (jnp.arange(top)[None, :] + offset_by) % top, axis=1)


def shares(number_of, total, limit, skew, full):
    loads = [(1 << 20) // math.isqrt(grade ** skew) + 1 for grade in range(1, number_of + 1)]
    largest = limit if full else min(limit, max(-(-total // number_of), total * loads[0] // sum(loads)))
    least = 1 if total - largest >= number_of - 1 else 0
    counts, surplus = [largest] + [least] * (number_of - 1), total - largest - least * (number_of - 1)
    while surplus > 0:
        free = [i for i in range(1, number_of) if counts[i] < largest] or [i for i in range(1, number_of) if counts[i] < limit]
        mass, budget = sum([loads[i] for i in free]), surplus
        for i in free:
            extra = min(limit - counts[i], max(1, budget * loads[i] // mass), surplus)
            counts[i] = counts[i] + extra
            surplus = surplus - extra
    return np.array(counts)


def scatter_about(own_key, shape, width, bound, shards=(), held_as=jnp.bfloat16):
    result = jax.random.normal(own_key, shape, jnp.float32) * width
    if len(shards) > 0:
        result = block_levels(own_key, shape, shards, -0.22, 0.18) * result
    return jnp.clip(result, min=-bound, max=bound).astype(held_as)


def setup_inputs(seed: int = 0) -> dict:
    key_of = jax.random.split(jax.random.key(seed), 5)
    tile_values = scatter_about(key_of[0], (TILES, BS, BS * BS), 1.0, 6.0, ((0, 512),))
    tile_owner_keys = jax.random.split(jax.random.fold_in(key_of[1], 1), TILES // TILES_DEV)
    tile_owner_turns = jax.random.permutation(jax.random.fold_in(key_of[1], 3), TILES // TILES_DEV)
    tile_owner = jax.vmap(lambda own, number: routed_block(jax.random.fold_in(key_of[1], 2), own, number, TILES_DEV, N_AO, 1, CAP, 2))(tile_owner_keys, tile_owner_turns).reshape((TILES, 1))
    tile_block = place_ends(jax.random.randint(key_of[2], (TILES,), 0, LB_DEV), jax.random.fold_in(key_of[2], 1), 0, LB_DEV - 1).astype(jnp.int32)
    coefficients = scatter_about(key_of[3], (NLAM, BS, 2 * NOCC), (TILES_DEV * BS) ** -0.5, 0.21875, ((0, 16),))
    return dict(tile_values=tile_values, tile_owner=tile_owner, tile_block=tile_block, coefficients=coefficients)


def aux_group(tile_group, block_group, coefficients):
    gathered = coefficients[block_group]
    transformed = jnp.einsum('rtlc,rtlmp->rmcp', gathered.astype(jnp.float32), tile_group.astype(jnp.float32)).astype(jnp.bfloat16)
    left_side = transformed[:, :, :NOCC, :].reshape(N_AO, BS, NOCC * BS)
    response = transformed[:, :, NOCC:, :].reshape(N_AO * BS, NOCC * BS)
    padded = jnp.pad(response, ((HW, HW), (0, 0)))
    window_index = jnp.arange(N_AO, dtype=jnp.int32)[:, None] * BS + jnp.arange(BS + 2 * HW, dtype=jnp.int32)[None, :]
    windows = padded[window_index]
    return jnp.einsum('rmk,rnk->rmn', left_side.astype(jnp.float32), windows.astype(jnp.float32))

def reference(tile_values, tile_owner, tile_block, coefficients):
    source_block = (tile_owner[:, 0] * LB_DEV + tile_block).astype(jnp.int32)
    grouped = tile_values.reshape(N_AUX, N_AO, TILES_DEV, BS, BS, BS)
    block_groups = source_block.reshape(N_AUX, N_AO, TILES_DEV)

    def one_group(pair):
        return aux_group(pair[0], pair[1], coefficients)
    partials = lax.map(one_group, (grouped, block_groups))
    factor = 1.0 / math.sqrt(NOCC * BS * N_AUX)
    total = lax.optimization_barrier(jnp.sum(partials, axis=0)) * factor
    return total.reshape(N_AO, BS * (BS + 2 * HW))
```

```python
import functools
import math

import jax
import jax.numpy as jnp
from jax import lax
from jax.experimental import pallas as pl
from jax.experimental.pallas import tpu as pltpu
from jax.sharding import PartitionSpec as P

X = 4
BS = 48
HW = 16
PB = 16
NN = (((1,), (0,)), ((), ()))
NT = (((1,), (1,)), ((), ()))


def dot(a, b, dims):
    return lax.dot_general(a, b, dims, preferred_element_type=jnp.float32)


def kernel(
    Y, Z, factor,
    owner_ref, block_ref, tiles_ref, coef_ref, out_ref,
    tiles, perm, tt, cg, picked, occ, rsp, halo, band, send1, recv1, send2, recv2, idx_v, idx_s,
    tile_sem, coef_sem, sis_send, sis_recv, ring_send, ring_recv, tt_send, tt_recv,
    idx_send, idx_recv, idx_sem, halo_send, halo_recv, s1_send, s1_recv, s2_send, s2_recv,
):
    aux, ao = lax.axis_index("aux"), lax.axis_index("ao")
    y, x = aux // X, aux % X
    z, core = ao // 2, ao % 2
    other = 1 - core
    held = coef_ref.shape[0]
    per = 2 * held
    half = Z // 2
    group = 2 * X
    spot = x * 2 + core

    def at_z(step):
        return {"aux": aux, "ao": lax.rem(z + step + Z, Z) * 2 + core}

    def at_group(step):
        there = lax.rem(spot + step, group)
        return {"aux": y * X + there // 2, "ao": z * 2 + there % 2}

    def at_y(step):
        return {"aux": lax.rem(y + step, Y) * X + x, "ao": ao}

    sister = {"aux": aux, "ao": z * 2 + other}

    def remote(src, dst, send, recv, where):
        return pltpu.make_async_remote_copy(
            src_ref=src, dst_ref=dst, send_sem=send, recv_sem=recv,
            device_id=where, device_id_type=pl.DeviceIdType.MESH,
        )

    tile_copy = pltpu.make_async_copy(tiles_ref, tiles, tile_sem)
    tile_copy.start()

    barrier = pltpu.get_barrier_semaphore()
    peers = [at_z(1), at_z(-1)] + [at_group(d) for d in range(1, group)] + [at_y(d) for d in range(1, Y)]
    for peer in peers:
        pl.semaphore_signal(barrier, inc=1, device_id=peer, device_id_type=pl.DeviceIdType.MESH)

    mine = ao * held
    local, swap = [], []
    for part in range(2):
        own = pl.ds(pl.multiple_of(part * 256 + core * 128, 128), 128)
        theirs = pl.ds(pl.multiple_of(part * 256 + other * 128, 128), 128)
        into = cg.at[pl.ds(mine, held), :, pl.ds(part * 128, 128)]
        local.append(pltpu.make_async_copy(coef_ref.at[:, :, own], into, coef_sem.at[part]))
        swap.append(remote(coef_ref.at[:, :, theirs], into, sis_send.at[part], sis_recv.at[part], sister))
    for copy in local:
        copy.start()

    lane = lax.broadcasted_iota(jnp.int32, (8, 128), 1)
    listed = jnp.zeros((8, 128), jnp.int32)
    for t in range(16):
        listed = jnp.where(lane == t, owner_ref[t] * held + block_ref[t], listed)
    idx_v[0] = listed

    pl.semaphore_wait(barrier, len(peers))
    for copy in swap:
        copy.start()
    idx_copy = remote(idx_v.at[0], idx_v.at[1], idx_send, idx_recv, sister)
    idx_copy.start()

    rows = lax.broadcasted_iota(jnp.int32, (768, 768), 0)
    want = (rows & 15) * BS + (rows >> 4)
    perm[...] = (lax.broadcasted_iota(jnp.int32, (768, 768), 1) == want).astype(jnp.bfloat16)

    for copy in local:
        copy.wait()
    for copy in swap:
        copy.wait()

    def ring(step):
        ups, downs = lax.rem(z - (step - 1) + Z, Z), lax.rem(z + (step - 1), Z)
        size = held if step == half else per
        up = cg.at[pl.ds(ups * per, size)]
        down = cg.at[pl.ds(downs * per + (per - size), size)]
        return [
            remote(up, up, ring_send.at[0, step - 1], ring_recv.at[0, step - 1], at_z(1)),
            remote(down, down, ring_send.at[1, step - 1], ring_recv.at[1, step - 1], at_z(-1)),
        ]

    def turn(part):
        rhs = tiles[:, :, part * 768:(part + 1) * 768].reshape(768, 768)

        def body(i, carry):
            start = pl.multiple_of(i * 256, 256)
            got = dot(perm[pl.ds(start, 256), :], rhs, NT).astype(jnp.bfloat16)
            tt[core, pl.ds(i * 16, 16), part * 16:(part + 1) * 16, :] = got.reshape(16, 16, 768)
            return carry

        lax.fori_loop(0, 3, body, 0)

    tt_copy = remote(tt.at[core], tt.at[core], tt_send, tt_recv, sister)
    for step in range(1, half + 1):
        copies = ring(step)
        for copy in copies:
            copy.start()
        if step == 1:
            tile_copy.wait()
            for part in range(3):
                turn(part)
            tt_copy.start()
        if step == 2:
            idx_copy.wait()
            fetch = pltpu.make_async_copy(idx_v.at[1], idx_s, idx_sem)
            fetch.start()
            fetch.wait()
        for copy in copies:
            copy.wait()
    tt_copy.wait()

    for t in range(16):
        picked[core, t * BS:(t + 1) * BS, :] = cg[owner_ref[t] * held + block_ref[t]]
        picked[other, t * BS:(t + 1) * BS, :] = cg[idx_s[0, t]]

    halos = []
    for b in range(BS // PB):
        ps = pl.ds(b * PB, PB)
        for r in range(2):
            right = picked[r]

            def body(i, carry):
                p = b * PB + i * 8
                got = dot(tt[r, pl.ds(p, 8)].reshape(8 * BS, 768), right, NN).astype(jnp.bfloat16)
                got = got.reshape(8, BS, 256)
                occ[pl.ds(p, 8), r * BS:(r + 1) * BS, :] = got[:, :, :128]
                rsp[pl.ds(p, 8), r * BS:(r + 1) * BS, :] = got[:, :, 128:]
                return carry

            lax.fori_loop(0, PB // 8, body, 0)
        down = remote(rsp.at[ps, 0:HW], halo.at[1, ps], halo_send.at[1, b], halo_recv.at[1, b], at_z(-1))
        up = remote(rsp.at[ps, 2 * BS - HW:2 * BS], halo.at[0, ps], halo_send.at[0, b], halo_recv.at[0, b], at_z(1))
        down.start()
        up.start()
        halos += [(down, up)]

    total = jnp.zeros((2 * BS, 2 * BS + 2 * HW), jnp.float32)
    for b in range(BS // PB):
        for copy in halos[b]:
            copy.wait()
        left, wide = [], []
        for p in range(b * PB, (b + 1) * PB):
            left.append(occ[p])
            wide.append(jnp.concatenate([halo[0, p], rsp[p], halo[1, p]], axis=0))
        total = total + dot(jnp.concatenate(left, axis=1), jnp.concatenate(wide, axis=1), NT)

    shape = (2 * BS, 2 * BS + 2 * HW)
    at_row, at_col = lax.broadcasted_iota(jnp.int32, shape, 0), lax.broadcasted_iota(jnp.int32, shape, 1)
    outside = jnp.logical_or(
        jnp.logical_and(z == 0, at_col < HW), jnp.logical_and(z == Z - 1, at_col >= 2 * BS + HW)
    )
    band[...] = jnp.where(outside, 0.0, total)

    for there in range(group):
        xx, c = there // 2, there % 2
        first = c * BS + 3 * (xx // 2)
        shift = BS * c
        if xx % 2 == 0:
            one, two = band[pl.ds(first, 8, stride=6), :], band[pl.ds(first + 1, 8, stride=6), :]
            a, b, cut = (128 - shift) % 128, (80 - shift) % 128, 80
        else:
            one, two = band[pl.ds(first + 1, 8, stride=6), :], band[pl.ds(first + 2, 8, stride=6), :]
            a, b, cut = (128 - shift - 40) % 128, (40 - shift) % 128, 40
        one = pltpu.roll(one, a, 1) if a else one
        two = pltpu.roll(two, b, 1) if b else two
        send1[there] = jnp.where(lane < cut, one, two)

    copies = []
    for d in range(1, group):
        there = lax.rem(spot + d, group)
        copies.append(remote(send1.at[there], recv1.at[d], s1_send.at[d], s1_recv.at[d], at_group(d)))
        copies[-1].start()
    partial = send1[spot]
    for d in range(1, group):
        copies[d - 1].wait()
        partial = partial + recv1[d]
    send2[...] = partial
    copies = []
    for d in range(1, Y):
        copies.append(remote(send2, recv2.at[d], s2_send.at[d], s2_recv.at[d], at_y(d)))
        copies[-1].start()
    for d in range(1, Y):
        copies[d - 1].wait()
        partial = partial + recv2[d]
    row = lax.broadcasted_iota(jnp.int32, (8, 128), 0)
    out_ref[...] = jnp.sum(jnp.where(row == y, partial, 0.0), axis=0, keepdims=True) * factor


def local(tile_values, tile_owner, tile_block, coefficients):
    n_aux, n_ao = lax.axis_size("aux"), lax.axis_size("ao")
    Y, Z = n_aux // X, n_ao // 2
    count = tile_values.shape[0]
    held = coefficients.shape[0]
    factor = 1.0 / math.sqrt(256 * BS * n_aux)
    bf, f32 = jnp.bfloat16, jnp.float32
    dma = pltpu.SemaphoreType.DMA
    got = pl.pallas_call(
        functools.partial(kernel, Y, Z, factor),
        out_shape=jax.ShapeDtypeStruct((1, 128), f32),
        in_specs=[
            pl.BlockSpec(memory_space=pltpu.SMEM),
            pl.BlockSpec(memory_space=pltpu.SMEM),
            pl.BlockSpec(memory_space=pl.ANY),
            pl.BlockSpec(memory_space=pl.ANY),
        ],
        out_specs=pl.BlockSpec(memory_space=pltpu.VMEM),
        scratch_shapes=[
            pltpu.VMEM((count, BS, BS * BS), bf),
            pltpu.VMEM((768, 768), bf),
            pltpu.VMEM((2, BS, BS, 768), bf),
            pltpu.VMEM((n_ao * held, BS, 256), bf),
            pltpu.VMEM((2, 768, 256), bf),
            pltpu.VMEM((BS, 2 * BS, 128), bf),
            pltpu.VMEM((BS, 2 * BS, 128), bf),
            pltpu.VMEM((2, BS, HW, 128), bf),
            pltpu.VMEM((2 * BS, 2 * BS + 2 * HW), f32),
            pltpu.VMEM((2 * X, 8, 128), f32),
            pltpu.VMEM((2 * X, 8, 128), f32),
            pltpu.VMEM((8, 128), f32),
            pltpu.VMEM((Y, 8, 128), f32),
            pltpu.VMEM((2, 8, 128), jnp.int32),
            pltpu.SMEM((8, 128), jnp.int32),
            dma, dma((2,)), dma((2,)), dma((2,)),
            dma((2, Z // 2)), dma((2, Z // 2)), dma, dma,
            dma, dma, dma,
            dma((2, BS // PB)), dma((2, BS // PB)),
            dma((2 * X,)), dma((2 * X,)), dma((Y,)), dma((Y,)),
        ],
        compiler_params=pltpu.CompilerParams(
            collective_id=0, has_side_effects=True, vmem_limit_bytes=48 * 1024 * 1024
        ),
        name="exchange",
    )(tile_owner.reshape(count), tile_block, tile_values, coefficients)
    return got[:, :BS * (BS + 2 * HW) // n_aux]


def solution(mesh):
    placed = (
        P(("aux", "ao"), None, None),
        P(("aux", "ao"), None),
        P(("aux", "ao")),
        P("ao", None, None),
    )
    return jax.shard_map(
        local, mesh=mesh, in_specs=placed, out_specs=P("ao", "aux"), check_vma=False
    )
```

```python
import functools
import math

import jax
import jax.numpy as jnp
from jax import lax
from jax.experimental import pallas as pl
from jax.experimental.pallas import tpu as pltpu
from jax.sharding import PartitionSpec as P

X = 4
BS = 48
HW = 16
PB = 8
SUBS = 4
NN = (((1,), (0,)), ((), ()))
NT = (((1,), (1,)), ((), ()))


def dot(a, b, dims):
    return lax.dot_general(a, b, dims, preferred_element_type=jnp.float32)


def kernel(
    Y, Z, factor,
    owner_hbm, block_hbm, tiles_ref, coef_ref, out_ref,
    owner_ref, block_ref,
    tiles, perm, tt, cg, picked, occ, rsp, halo, band, send1, recv1, send2, recv2, idx_v, idx_s,
    list_sem, tile_sem, coef_sem, sis_send, sis_recv, ring_send, ring_recv, tt_send, tt_recv,
    idx_send, idx_recv, idx_sem, halo_send, halo_recv, s1_send, s1_recv, s2_send, s2_recv,
):
    aux, ao = lax.axis_index("aux"), lax.axis_index("ao")
    y, x = aux // X, aux % X
    z, core = ao // 2, ao % 2
    other = 1 - core
    held = coef_ref.shape[0]
    per = 2 * held
    half = Z // 2
    group = 2 * X
    spot = x * 2 + core

    def at_z(step):
        return {"aux": aux, "ao": lax.rem(z + step + Z, Z) * 2 + core}

    def at_group(step):
        there = lax.rem(spot + step, group)
        return {"aux": y * X + there // 2, "ao": z * 2 + there % 2}

    def at_y(step):
        return {"aux": lax.rem(y + step, Y) * X + x, "ao": ao}

    sister = {"aux": aux, "ao": z * 2 + other}

    def remote(src, dst, send, recv, where):
        return pltpu.make_async_remote_copy(
            src_ref=src, dst_ref=dst, send_sem=send, recv_sem=recv,
            device_id=where, device_id_type=pl.DeviceIdType.MESH,
        )

    tile_copy = pltpu.make_async_copy(tiles_ref, tiles, tile_sem)
    tile_copy.start()
    lists = [
        pltpu.make_async_copy(owner_hbm, owner_ref, list_sem.at[0]),
        pltpu.make_async_copy(block_hbm, block_ref, list_sem.at[1]),
    ]
    for copy in lists:
        copy.start()

    barrier = pltpu.get_barrier_semaphore()
    peers = [at_z(1), at_z(-1)] + [at_group(d) for d in range(1, group)] + [at_y(d) for d in range(1, Y)]
    for peer in peers:
        pl.semaphore_signal(barrier, inc=1, device_id=peer, device_id_type=pl.DeviceIdType.MESH)

    mine = ao * held
    local, swap = [], []
    for part in range(2):
        own = pl.ds(pl.multiple_of(part * 256 + core * 128, 128), 128)
        theirs = pl.ds(pl.multiple_of(part * 256 + other * 128, 128), 128)
        into = cg.at[pl.ds(mine, held), :, pl.ds(part * 128, 128)]
        local.append(pltpu.make_async_copy(coef_ref.at[:, :, own], into, coef_sem.at[part]))
        swap.append(remote(coef_ref.at[:, :, theirs], into, sis_send.at[part], sis_recv.at[part], sister))
    for copy in local:
        copy.start()

    rows = lax.broadcasted_iota(jnp.int32, (768, 768), 0)
    want = (rows & 15) * BS + (rows >> 4)
    perm[...] = (lax.broadcasted_iota(jnp.int32, (768, 768), 1) == want).astype(jnp.bfloat16)

    pl.semaphore_wait(barrier, len(peers))
    for copy in swap:
        copy.start()

    size = per // SUBS

    def hop(step, sub):
        spot_in = lax.rem(sub + core * (SUBS // 2), SUBS) * size
        ups, downs = lax.rem(z - (step - 1) + Z, Z), lax.rem(z + (step - 1), Z)
        up, down = cg.at[pl.ds(ups * per + spot_in, size)], cg.at[pl.ds(downs * per + spot_in, size)]
        copies = []
        if step < half or sub % 2 == 0:
            copies.append(remote(up, up, ring_send.at[0, step - 1, sub], ring_recv.at[0, step - 1, sub], at_z(1)))
        if step < half or sub % 2 == 1:
            copies.append(remote(down, down, ring_send.at[1, step - 1, sub], ring_recv.at[1, step - 1, sub], at_z(-1)))
        for copy in copies:
            copy.start()
        return copies

    chains = []
    for copy in local:
        copy.wait()
    for sub in range(SUBS // 2):
        chains.append([hop(1, sub)])
    for copy in swap:
        copy.wait()
    for sub in range(SUBS // 2, SUBS):
        chains.append([hop(1, sub)])

    lane = lax.broadcasted_iota(jnp.int32, (8, 128), 1)
    listed = jnp.zeros((8, 128), jnp.int32)
    for copy in lists:
        copy.wait()
    for t in range(16):
        listed = jnp.where(lane == t, owner_ref[t] * held + block_ref[t], listed)
    idx_v[0] = listed
    idx_copy = remote(idx_v.at[0], idx_v.at[1], idx_send, idx_recv, sister)
    idx_copy.start()

    def turn(part):
        rhs = tiles[:, :, part * 768:(part + 1) * 768].reshape(768, 768)

        def body(i, carry):
            start = pl.multiple_of(i * 256, 256)
            got = dot(perm[pl.ds(start, 256), :], rhs, NT).astype(jnp.bfloat16)
            tt[core, pl.ds(i * 16, 16), part * 16:(part + 1) * 16, :] = got.reshape(16, 16, 768)
            return carry

        lax.fori_loop(0, 3, body, 0)

    tt_copy = remote(tt.at[core], tt.at[core], tt_send, tt_recv, sister)
    tile_copy.wait()
    for part in range(3):
        turn(part)
    tt_copy.start()
    for step in range(2, half + 1):
        for sub in range(SUBS):
            for copy in chains[sub][-1]:
                copy.wait_recv()
            chains[sub].append(hop(step, sub))
        if step == 2:
            idx_copy.wait()
            fetch = pltpu.make_async_copy(idx_v.at[1], idx_s, idx_sem)
            fetch.start()
            fetch.wait()
    for sub in range(SUBS):
        for copy in chains[sub][-1]:
            copy.wait_recv()
    for chain in chains:
        for copies in chain:
            for copy in copies:
                copy.wait_send()
    tt_copy.wait()

    for t in range(16):
        picked[core, t * BS:(t + 1) * BS, :] = cg[owner_ref[t] * held + block_ref[t]]
        picked[other, t * BS:(t + 1) * BS, :] = cg[idx_s[0, t]]

    halos = []
    for b in range(BS // PB):
        ps = pl.ds(b * PB, PB)
        for r in range(2):
            right = picked[r]

            def body(i, carry):
                p = b * PB + i * 8
                got = dot(tt[r, pl.ds(p, 8)].reshape(8 * BS, 768), right, NN).astype(jnp.bfloat16)
                got = got.reshape(8, BS, 256)
                occ[pl.ds(p, 8), r * BS:(r + 1) * BS, :] = got[:, :, :128]
                rsp[pl.ds(p, 8), r * BS:(r + 1) * BS, :] = got[:, :, 128:]
                return carry

            lax.fori_loop(0, PB // 8, body, 0)
        down = remote(rsp.at[ps, 0:HW], halo.at[1, ps], halo_send.at[1, b], halo_recv.at[1, b], at_z(-1))
        up = remote(rsp.at[ps, 2 * BS - HW:2 * BS], halo.at[0, ps], halo_send.at[0, b], halo_recv.at[0, b], at_z(1))
        down.start()
        up.start()
        halos += [(down, up)]

    total = jnp.zeros((2 * BS, 2 * BS + 2 * HW), jnp.float32)
    for b in range(BS // PB):
        for copy in halos[b]:
            copy.wait()
        left, wide = [], []
        for p in range(b * PB, (b + 1) * PB):
            left.append(occ[p])
            wide.append(jnp.concatenate([halo[0, p], rsp[p], halo[1, p]], axis=0))
        total = total + dot(jnp.concatenate(left, axis=1), jnp.concatenate(wide, axis=1), NT)

    shape = (2 * BS, 2 * BS + 2 * HW)
    at_row, at_col = lax.broadcasted_iota(jnp.int32, shape, 0), lax.broadcasted_iota(jnp.int32, shape, 1)
    outside = jnp.logical_or(
        jnp.logical_and(z == 0, at_col < HW), jnp.logical_and(z == Z - 1, at_col >= 2 * BS + HW)
    )
    band[...] = jnp.where(outside, 0.0, total)

    for there in range(group):
        xx, c = there // 2, there % 2
        first = c * BS + 3 * (xx // 2)
        shift = BS * c
        if xx % 2 == 0:
            one, two = band[pl.ds(first, 8, stride=6), :], band[pl.ds(first + 1, 8, stride=6), :]
            a, b, cut = (128 - shift) % 128, (80 - shift) % 128, 80
        else:
            one, two = band[pl.ds(first + 1, 8, stride=6), :], band[pl.ds(first + 2, 8, stride=6), :]
            a, b, cut = (128 - shift - 40) % 128, (40 - shift) % 128, 40
        one = pltpu.roll(one, a, 1) if a else one
        two = pltpu.roll(two, b, 1) if b else two
        send1[there] = jnp.where(lane < cut, one, two)

    copies = []
    for d in range(1, group):
        there = lax.rem(spot + d, group)
        copies.append(remote(send1.at[there], recv1.at[d], s1_send.at[d], s1_recv.at[d], at_group(d)))
        copies[-1].start()
    partial = send1[spot]
    for d in range(1, group):
        copies[d - 1].wait()
        partial = partial + recv1[d]
    send2[...] = partial
    copies = []
    for d in range(1, Y):
        copies.append(remote(send2, recv2.at[d], s2_send.at[d], s2_recv.at[d], at_y(d)))
        copies[-1].start()
    for d in range(1, Y):
        copies[d - 1].wait()
        partial = partial + recv2[d]
    row = lax.broadcasted_iota(jnp.int32, (8, 128), 0)
    out_ref[...] = jnp.sum(jnp.where(row == y, partial, 0.0), axis=0, keepdims=True) * factor


def local(tile_values, tile_owner, tile_block, coefficients):
    n_aux, n_ao = lax.axis_size("aux"), lax.axis_size("ao")
    Y, Z = n_aux // X, n_ao // 2
    count = tile_values.shape[0]
    held = coefficients.shape[0]
    factor = 1.0 / math.sqrt(256 * BS * n_aux)
    bf, f32 = jnp.bfloat16, jnp.float32
    dma = pltpu.SemaphoreType.DMA
    got = pl.pallas_call(
        functools.partial(kernel, Y, Z, factor),
        out_shape=jax.ShapeDtypeStruct((1, 128), f32),
        in_specs=[
            pl.BlockSpec(memory_space=pltpu.HBM),
            pl.BlockSpec(memory_space=pltpu.HBM),
            pl.BlockSpec(memory_space=pltpu.HBM),
            pl.BlockSpec(memory_space=pltpu.HBM),
        ],
        out_specs=pl.BlockSpec(memory_space=pltpu.VMEM),
        scratch_shapes=[
            pltpu.SMEM((count,), jnp.int32),
            pltpu.SMEM((count,), jnp.int32),
            pltpu.VMEM((count, BS, BS * BS), bf),
            pltpu.VMEM((768, 768), bf),
            pltpu.VMEM((2, BS, BS, 768), bf),
            pltpu.VMEM((n_ao * held, BS, 256), bf),
            pltpu.VMEM((2, 768, 256), bf),
            pltpu.VMEM((BS, 2 * BS, 128), bf),
            pltpu.VMEM((BS, 2 * BS, 128), bf),
            pltpu.VMEM((2, BS, HW, 128), bf),
            pltpu.VMEM((2 * BS, 2 * BS + 2 * HW), f32),
            pltpu.VMEM((2 * X, 8, 128), f32),
            pltpu.VMEM((2 * X, 8, 128), f32),
            pltpu.VMEM((8, 128), f32),
            pltpu.VMEM((Y, 8, 128), f32),
            pltpu.VMEM((2, 8, 128), jnp.int32),
            pltpu.SMEM((8, 128), jnp.int32),
            dma((2,)), dma, dma((2,)), dma((2,)), dma((2,)),
            dma((2, Z // 2, SUBS)), dma((2, Z // 2, SUBS)), dma, dma,
            dma, dma, dma,
            dma((2, BS // PB)), dma((2, BS // PB)),
            dma((2 * X,)), dma((2 * X,)), dma((Y,)), dma((Y,)),
        ],
        compiler_params=pltpu.CompilerParams(
            collective_id=0, has_side_effects=True, vmem_limit_bytes=60 * 1024 * 1024
        ),
        name="exchange",
    )(tile_owner.reshape(count), tile_block, tile_values, coefficients)
    return got[:, :BS * (BS + 2 * HW) // n_aux]


def solution(mesh):
    placed = (
        P(("aux", "ao"), None, None),
        P(("aux", "ao"), None),
        P(("aux", "ao")),
        P("ao", None, None),
    )
    return jax.shard_map(
        local, mesh=mesh, in_specs=placed, out_specs=P("ao", "aux"), check_vma=False
    )
```

```python
import functools
import math

import jax
import jax.numpy as jnp
from jax import lax
from jax.experimental import pallas as pl
from jax.experimental.pallas import tpu as pltpu
from jax.sharding import PartitionSpec as P

X = 4
BS = 48
HW = 16
PB = 8
SUBS = 4
NN = (((1,), (0,)), ((), ()))
NT = (((1,), (1,)), ((), ()))


def dot(a, b, dims):
    return lax.dot_general(a, b, dims, preferred_element_type=jnp.float32)


def kernel(
    Y, Z, factor,
    owner_hbm, block_hbm, tiles_ref, coef_ref, out_ref,
    owner_ref, block_ref,
    tiles, perm, tt, cg, picked, occ, rsp, halo, band, send1, recv1, send2, recv2, idx_v, idx_s,
    list_sem, tile_sem, coef_sem, sis_send, sis_recv, ring_send, ring_recv, side_send, side_recv, tt_send, tt_recv,
    idx_send, idx_recv, idx_sem, halo_send, halo_recv, s1_send, s1_recv, s2_send, s2_recv,
):
    aux, ao = lax.axis_index("aux"), lax.axis_index("ao")
    y, x = aux // X, aux % X
    z, core = ao // 2, ao % 2
    other = 1 - core
    held = coef_ref.shape[0]
    per = 2 * held
    half = Z // 2
    group = 2 * X
    spot = x * 2 + core

    def at_z(step):
        return {"aux": aux, "ao": lax.rem(z + step + Z, Z) * 2 + core}

    def at_group(step):
        there = lax.rem(spot + step, group)
        return {"aux": y * X + there // 2, "ao": z * 2 + there % 2}

    def at_y(step):
        return {"aux": lax.rem(y + step, Y) * X + x, "ao": ao}

    sister = {"aux": aux, "ao": z * 2 + other}

    def remote(src, dst, send, recv, where):
        return pltpu.make_async_remote_copy(
            src_ref=src, dst_ref=dst, send_sem=send, recv_sem=recv,
            device_id=where, device_id_type=pl.DeviceIdType.MESH,
        )

    tile_copy = pltpu.make_async_copy(tiles_ref, tiles, tile_sem)
    tile_copy.start()
    lists = [
        pltpu.make_async_copy(owner_hbm, owner_ref, list_sem.at[0]),
        pltpu.make_async_copy(block_hbm, block_ref, list_sem.at[1]),
    ]
    for copy in lists:
        copy.start()

    barrier = pltpu.get_barrier_semaphore()
    peers = [at_z(1), at_z(-1)] + [at_group(d) for d in range(1, group)] + [at_y(d) for d in range(1, Y)]
    for peer in peers:
        pl.semaphore_signal(barrier, inc=1, device_id=peer, device_id_type=pl.DeviceIdType.MESH)

    mine = ao * held
    local, swap = [], []
    for part in range(2):
        own = pl.ds(pl.multiple_of(part * 256 + core * 128, 128), 128)
        theirs = pl.ds(pl.multiple_of(part * 256 + other * 128, 128), 128)
        into = cg.at[pl.ds(mine, held), :, pl.ds(part * 128, 128)]
        local.append(pltpu.make_async_copy(coef_ref.at[:, :, own], into, coef_sem.at[part]))
        swap.append(remote(coef_ref.at[:, :, theirs], into, sis_send.at[part], sis_recv.at[part], sister))
    for copy in local:
        copy.start()

    rows = lax.broadcasted_iota(jnp.int32, (768, 768), 0)
    want = (rows & 15) * BS + (rows >> 4)
    perm[...] = (lax.broadcasted_iota(jnp.int32, (768, 768), 1) == want).astype(jnp.bfloat16)

    pl.semaphore_wait(barrier, len(peers))
    for copy in swap:
        copy.start()

    size = held // SUBS
    odd = x % 2

    def piece(slot, sub):
        part = lax.rem(sub // (SUBS // 2) + core, 2)
        start = part * held + odd * (held // 2) + sub % (SUBS // 2) * size
        return cg.at[pl.ds(lax.rem(slot + Z, Z) * per + start, size)]

    def beside(sub):
        part = lax.rem(sub // (SUBS // 2) + core, 2)
        step = (1 - 2 * odd) * (1 - 2 * part)
        return {"aux": y * X + lax.rem(x + step + X, X), "ao": ao}

    def share(step, sub):
        slots = [z - step, z + step] if step < half else [z + step]
        copies = []
        for i, slot in enumerate(slots):
            ref = piece(slot, sub)
            copies.append(remote(ref, ref, side_send.at[i, step - 1, sub], side_recv.at[i, step - 1, sub], beside(sub)))
            copies[-1].start()
        return copies

    def hop(step, sub):
        up, down = piece(z - (step - 1), sub), piece(z + (step - 1), sub)
        copies = []
        if step < half or sub % 2 == 0:
            copies.append(remote(up, up, ring_send.at[0, step - 1, sub], ring_recv.at[0, step - 1, sub], at_z(1)))
        if step < half or sub % 2 == 1:
            copies.append(remote(down, down, ring_send.at[1, step - 1, sub], ring_recv.at[1, step - 1, sub], at_z(-1)))
        for copy in copies:
            copy.start()
        return copies

    chains = []
    for copy in local:
        copy.wait()
    for sub in range(SUBS // 2):
        chains.append([hop(1, sub)])
    for copy in swap:
        copy.wait()
    for sub in range(SUBS // 2, SUBS):
        chains.append([hop(1, sub)])

    lane = lax.broadcasted_iota(jnp.int32, (8, 128), 1)
    listed = jnp.zeros((8, 128), jnp.int32)
    for copy in lists:
        copy.wait()
    for t in range(16):
        listed = jnp.where(lane == t, owner_ref[t] * held + block_ref[t], listed)
    idx_v[0] = listed
    idx_copy = remote(idx_v.at[0], idx_v.at[1], idx_send, idx_recv, sister)
    idx_copy.start()

    def turn(part):
        rhs = tiles[:, :, part * 768:(part + 1) * 768].reshape(768, 768)

        def body(i, carry):
            start = pl.multiple_of(i * 256, 256)
            got = dot(perm[pl.ds(start, 256), :], rhs, NT).astype(jnp.bfloat16)
            tt[core, pl.ds(i * 16, 16), part * 16:(part + 1) * 16, :] = got.reshape(16, 16, 768)
            return carry

        lax.fori_loop(0, 3, body, 0)

    tt_copy = remote(tt.at[core], tt.at[core], tt_send, tt_recv, sister)
    tile_copy.wait()
    for part in range(3):
        turn(part)
    tt_copy.start()
    sides = []
    for step in range(2, half + 1):
        for sub in range(SUBS):
            for copy in chains[sub][-1]:
                copy.wait_recv()
            chains[sub].append(hop(step, sub))
            sides += share(step - 1, sub)
        if step == 2:
            idx_copy.wait()
            fetch = pltpu.make_async_copy(idx_v.at[1], idx_s, idx_sem)
            fetch.start()
            fetch.wait()
    for sub in range(SUBS):
        for copy in chains[sub][-1]:
            copy.wait_recv()
        sides += share(half, sub)
    for copy in sides:
        copy.wait_recv()
    for copy in sides:
        copy.wait_send()
    for chain in chains:
        for copies in chain:
            for copy in copies:
                copy.wait_send()
    tt_copy.wait()

    for t in range(16):
        picked[core, t * BS:(t + 1) * BS, :] = cg[owner_ref[t] * held + block_ref[t]]
        picked[other, t * BS:(t + 1) * BS, :] = cg[idx_s[0, t]]

    halos = []
    for b in range(BS // PB):
        ps = pl.ds(b * PB, PB)
        for r in range(2):
            right = picked[r]

            def body(i, carry):
                p = b * PB + i * 8
                got = dot(tt[r, pl.ds(p, 8)].reshape(8 * BS, 768), right, NN).astype(jnp.bfloat16)
                got = got.reshape(8, BS, 256)
                occ[pl.ds(p, 8), r * BS:(r + 1) * BS, :] = got[:, :, :128]
                rsp[pl.ds(p, 8), r * BS:(r + 1) * BS, :] = got[:, :, 128:]
                return carry

            lax.fori_loop(0, PB // 8, body, 0)
        down = remote(rsp.at[ps, 0:HW], halo.at[1, ps], halo_send.at[1, b], halo_recv.at[1, b], at_z(-1))
        up = remote(rsp.at[ps, 2 * BS - HW:2 * BS], halo.at[0, ps], halo_send.at[0, b], halo_recv.at[0, b], at_z(1))
        down.start()
        up.start()
        halos += [(down, up)]

    total = jnp.zeros((2 * BS, 2 * BS + 2 * HW), jnp.float32)
    for b in range(BS // PB):
        for copy in halos[b]:
            copy.wait()
        left, wide = [], []
        for p in range(b * PB, (b + 1) * PB):
            left.append(occ[p])
            wide.append(jnp.concatenate([halo[0, p], rsp[p], halo[1, p]], axis=0))
        total = total + dot(jnp.concatenate(left, axis=1), jnp.concatenate(wide, axis=1), NT)

    shape = (2 * BS, 2 * BS + 2 * HW)
    at_row, at_col = lax.broadcasted_iota(jnp.int32, shape, 0), lax.broadcasted_iota(jnp.int32, shape, 1)
    outside = jnp.logical_or(
        jnp.logical_and(z == 0, at_col < HW), jnp.logical_and(z == Z - 1, at_col >= 2 * BS + HW)
    )
    band[...] = jnp.where(outside, 0.0, total)

    for there in range(group):
        xx, c = there // 2, there % 2
        first = c * BS + 3 * (xx // 2)
        shift = BS * c
        if xx % 2 == 0:
            one, two = band[pl.ds(first, 8, stride=6), :], band[pl.ds(first + 1, 8, stride=6), :]
            a, b, cut = (128 - shift) % 128, (80 - shift) % 128, 80
        else:
            one, two = band[pl.ds(first + 1, 8, stride=6), :], band[pl.ds(first + 2, 8, stride=6), :]
            a, b, cut = (128 - shift - 40) % 128, (40 - shift) % 128, 40
        one = pltpu.roll(one, a, 1) if a else one
        two = pltpu.roll(two, b, 1) if b else two
        send1[there] = jnp.where(lane < cut, one, two)

    copies = []
    for d in range(1, group):
        there = lax.rem(spot + d, group)
        copies.append(remote(send1.at[there], recv1.at[d], s1_send.at[d], s1_recv.at[d], at_group(d)))
        copies[-1].start()
    partial = send1[spot]
    for d in range(1, group):
        copies[d - 1].wait()
        partial = partial + recv1[d]
    send2[...] = partial
    copies = []
    for d in range(1, Y):
        copies.append(remote(send2, recv2.at[d], s2_send.at[d], s2_recv.at[d], at_y(d)))
        copies[-1].start()
    for d in range(1, Y):
        copies[d - 1].wait()
        partial = partial + recv2[d]
    row = lax.broadcasted_iota(jnp.int32, (8, 128), 0)
    out_ref[...] = jnp.sum(jnp.where(row == y, partial, 0.0), axis=0, keepdims=True) * factor


def local(tile_values, tile_owner, tile_block, coefficients):
    n_aux, n_ao = lax.axis_size("aux"), lax.axis_size("ao")
    Y, Z = n_aux // X, n_ao // 2
    count = tile_values.shape[0]
    held = coefficients.shape[0]
    factor = 1.0 / math.sqrt(256 * BS * n_aux)
    bf, f32 = jnp.bfloat16, jnp.float32
    dma = pltpu.SemaphoreType.DMA
    got = pl.pallas_call(
        functools.partial(kernel, Y, Z, factor),
        out_shape=jax.ShapeDtypeStruct((1, 128), f32),
        in_specs=[
            pl.BlockSpec(memory_space=pltpu.HBM),
            pl.BlockSpec(memory_space=pltpu.HBM),
            pl.BlockSpec(memory_space=pltpu.HBM),
            pl.BlockSpec(memory_space=pltpu.HBM),
        ],
        out_specs=pl.BlockSpec(memory_space=pltpu.VMEM),
        scratch_shapes=[
            pltpu.SMEM((count,), jnp.int32),
            pltpu.SMEM((count,), jnp.int32),
            pltpu.VMEM((count, BS, BS * BS), bf),
            pltpu.VMEM((768, 768), bf),
            pltpu.VMEM((2, BS, BS, 768), bf),
            pltpu.VMEM((n_ao * held, BS, 256), bf),
            pltpu.VMEM((2, 768, 256), bf),
            pltpu.VMEM((BS, 2 * BS, 128), bf),
            pltpu.VMEM((BS, 2 * BS, 128), bf),
            pltpu.VMEM((2, BS, HW, 128), bf),
            pltpu.VMEM((2 * BS, 2 * BS + 2 * HW), f32),
            pltpu.VMEM((2 * X, 8, 128), f32),
            pltpu.VMEM((2 * X, 8, 128), f32),
            pltpu.VMEM((8, 128), f32),
            pltpu.VMEM((Y, 8, 128), f32),
            pltpu.VMEM((2, 8, 128), jnp.int32),
            pltpu.SMEM((8, 128), jnp.int32),
            dma((2,)), dma, dma((2,)), dma((2,)), dma((2,)),
            dma((2, Z // 2, SUBS)), dma((2, Z // 2, SUBS)), dma((2, Z // 2, SUBS)), dma((2, Z // 2, SUBS)), dma, dma,
            dma, dma, dma,
            dma((2, BS // PB)), dma((2, BS // PB)),
            dma((2 * X,)), dma((2 * X,)), dma((Y,)), dma((Y,)),
        ],
        compiler_params=pltpu.CompilerParams(
            collective_id=0, has_side_effects=True, vmem_limit_bytes=60 * 1024 * 1024
        ),
        name="exchange",
    )(tile_owner.reshape(count), tile_block, tile_values, coefficients)
    return got[:, :BS * (BS + 2 * HW) // n_aux]


def solution(mesh):
    placed = (
        P(("aux", "ao"), None, None),
        P(("aux", "ao"), None),
        P(("aux", "ao")),
        P("ao", None, None),
    )
    return jax.shard_map(
        local, mesh=mesh, in_specs=placed, out_specs=P("ao", "aux"), check_vma=False
    )
```

```python
import functools
import math

import jax
import jax.numpy as jnp
from jax import lax
from jax.experimental import pallas as pl
from jax.experimental.pallas import tpu as pltpu
from jax.sharding import PartitionSpec as P

X = 4
BS = 48
HW = 16
PB = 8
SUBS = 4
NN = (((1,), (0,)), ((), ()))
NT = (((1,), (1,)), ((), ()))


def dot(a, b, dims):
    return lax.dot_general(a, b, dims, preferred_element_type=jnp.float32)


def kernel(
    Y, Z, factor,
    owner_hbm, block_hbm, tiles_ref, coef_ref, out_ref,
    owner_ref, block_ref,
    tiles, perm, tt, cg, picked, occ, rsp, halo, band, parts, cross_in, rows_out, rows_in, idx_v, idx_s,
    list_sem, tile_sem, coef_sem, sis_send, sis_recv, ring_send, ring_recv, side_send, side_recv, far_send, far_recv, tt_send, tt_recv,
    idx_send, idx_recv, idx_sem, halo_send, halo_recv, s1_send, s1_recv, s2_send, s2_recv,
):
    aux, ao = lax.axis_index("aux"), lax.axis_index("ao")
    y, x = aux // X, aux % X
    z, core = ao // 2, ao % 2
    other = 1 - core
    held = coef_ref.shape[0]
    per = 2 * held
    half = Z // 2
    plane = [(dx, dy) for dx in range(X) for dy in range(Y) if dx or dy]
    plane.sort(key=lambda at: -(min(at[0], X - at[0]) + min(at[1], Y - at[1])))

    def at_z(step):
        return {"aux": aux, "ao": lax.rem(z + step + Z, Z) * 2 + core}

    def at_plane(dx, dy):
        return {"aux": lax.rem(y + dy, Y) * X + lax.rem(x + dx, X), "ao": ao}

    sister = {"aux": aux, "ao": z * 2 + other}

    def remote(src, dst, send, recv, where):
        return pltpu.make_async_remote_copy(
            src_ref=src, dst_ref=dst, send_sem=send, recv_sem=recv,
            device_id=where, device_id_type=pl.DeviceIdType.MESH,
        )

    tile_copy = pltpu.make_async_copy(tiles_ref, tiles, tile_sem)
    tile_copy.start()
    lists = [
        pltpu.make_async_copy(owner_hbm, owner_ref, list_sem.at[0]),
        pltpu.make_async_copy(block_hbm, block_ref, list_sem.at[1]),
    ]
    for copy in lists:
        copy.start()

    barrier = pltpu.get_barrier_semaphore()
    peers = [at_plane(dx, dy) for dx, dy in plane] + [at_z(half), at_z(1), at_z(-1), sister]
    for peer in peers:
        pl.semaphore_signal(barrier, inc=1, device_id=peer, device_id_type=pl.DeviceIdType.MESH)

    mine = ao * held
    local, swap = [], []
    for part in range(2):
        own = pl.ds(pl.multiple_of(part * 256 + core * 128, 128), 128)
        theirs = pl.ds(pl.multiple_of(part * 256 + other * 128, 128), 128)
        into = cg.at[pl.ds(mine, held), :, pl.ds(part * 128, 128)]
        local.append(pltpu.make_async_copy(coef_ref.at[:, :, own], into, coef_sem.at[part]))
        swap.append(remote(coef_ref.at[:, :, theirs], into, sis_send.at[part], sis_recv.at[part], sister))
    for copy in local:
        copy.start()

    rows = lax.broadcasted_iota(jnp.int32, (768, 768), 0)
    want = (rows & 15) * BS + (rows >> 4)
    perm[...] = (lax.broadcasted_iota(jnp.int32, (768, 768), 1) == want).astype(jnp.bfloat16)

    pl.semaphore_wait(barrier, len(peers))
    for copy in swap:
        copy.start()

    size = held // SUBS
    odd = x % 2

    def piece(slot, sub):
        part = lax.rem(sub // (SUBS // 2) + core, 2)
        start = part * held + odd * (held // 2) + sub % (SUBS // 2) * size
        return cg.at[pl.ds(lax.rem(slot + Z, Z) * per + start, size)]

    def beside(sub):
        part = lax.rem(sub // (SUBS // 2) + core, 2)
        step = (1 - 2 * odd) * (1 - 2 * part)
        return {"aux": y * X + lax.rem(x + step + X, X), "ao": ao}

    def share(step, sub):
        slots = [z - step, z + step] if step < half else [z + step]
        copies = []
        for i, slot in enumerate(slots):
            ref = piece(slot, sub)
            copies.append(remote(ref, ref, side_send.at[i, step - 1, sub], side_recv.at[i, step - 1, sub], beside(sub)))
            copies[-1].start()
        return copies

    def hop(step, sub):
        up, down = piece(z - (step - 1), sub), piece(z + (step - 1), sub)
        copies = [
            remote(up, up, ring_send.at[0, step - 1, sub], ring_recv.at[0, step - 1, sub], at_z(1)),
            remote(down, down, ring_send.at[1, step - 1, sub], ring_recv.at[1, step - 1, sub], at_z(-1)),
        ]
        for copy in copies:
            copy.start()
        return copies

    def eighth(slot):
        start = y // (Y // 2) * held + odd * (held // 2) + y % (Y // 2)
        return cg.at[pl.ds(lax.rem(slot + Z, Z) * per + start, 1)]

    chains = []
    for copy in local:
        copy.wait()
    for sub in range(SUBS // 2):
        chains.append([hop(1, sub)])
    for copy in swap:
        copy.wait()
    far = remote(eighth(z), eighth(z), far_send.at[0], far_recv.at[0], at_z(half))
    far.start()
    for sub in range(SUBS // 2, SUBS):
        chains.append([hop(1, sub)])

    lane = lax.broadcasted_iota(jnp.int32, (8, 128), 1)
    listed = jnp.zeros((8, 128), jnp.int32)
    for copy in lists:
        copy.wait()
    for t in range(16):
        listed = jnp.where(lane == t, owner_ref[t] * held + block_ref[t], listed)
    idx_v[0] = listed
    idx_copy = remote(idx_v.at[0], idx_v.at[1], idx_send, idx_recv, sister)
    idx_copy.start()

    def turn(part):
        rhs = tiles[:, :, part * 768:(part + 1) * 768].reshape(768, 768)

        def body(i, carry):
            start = pl.multiple_of(i * 256, 256)
            got = dot(perm[pl.ds(start, 256), :], rhs, NT).astype(jnp.bfloat16)
            tt[core, pl.ds(i * 16, 16), part * 16:(part + 1) * 16, :] = got.reshape(16, 16, 768)
            return carry

        lax.fori_loop(0, 3, body, 0)

    turned = []

    def turn_next():
        part = len(turned)
        turn(part)
        ref = tt.at[core, :, part * 16:(part + 1) * 16]
        turned.append(remote(ref, ref, tt_send.at[part], tt_recv.at[part], sister))
        turned[-1].start()

    sides, rounds = [], []
    for step in range(2, half):
        for sub in range(SUBS):
            for copy in chains[sub][-1]:
                copy.wait_recv()
            chains[sub].append(hop(step, sub))
            sides += share(step - 1, sub)
        if step == 2:
            far.wait_recv()
            ref = eighth(z + half)
            for dy in sorted(range(1, Y), key=lambda dy: -min(dy, Y - dy)):
                rounds.append(remote(ref, ref, far_send.at[dy], far_recv.at[dy], at_plane(0, dy)))
                rounds[-1].start()
            tile_copy.wait()
        turn_next()
    idx_copy.wait()
    fetch = pltpu.make_async_copy(idx_v.at[1], idx_s, idx_sem)
    fetch.start()
    turn_next()
    for copy in rounds:
        copy.wait_recv()
    for sub in range(SUBS):
        sides += share(half, sub)
    for sub in range(SUBS):
        for copy in chains[sub][-1]:
            copy.wait_recv()
        sides += share(half - 1, sub)
    fetch.wait()
    for copy in turned:
        copy.wait()
    for copy in sides:
        copy.wait_recv()
    for copy in sides + rounds + [far]:
        copy.wait_send()
    for chain in chains:
        for copies in chain:
            for copy in copies:
                copy.wait_send()

    for t in range(16):
        picked[core, t * BS:(t + 1) * BS, :] = cg[owner_ref[t] * held + block_ref[t]]
        picked[other, t * BS:(t + 1) * BS, :] = cg[idx_s[0, t]]

    halos = []
    for b in range(BS // PB):
        ps = pl.ds(b * PB, PB)
        for r in range(2):
            right = picked[r]

            def body(i, carry):
                p = b * PB + i * 8
                got = dot(tt[r, pl.ds(p, 8)].reshape(8 * BS, 768), right, NN).astype(jnp.bfloat16)
                got = got.reshape(8, BS, 256)
                occ[pl.ds(p, 8), r * BS:(r + 1) * BS, :] = got[:, :, :128]
                rsp[pl.ds(p, 8), r * BS:(r + 1) * BS, :] = got[:, :, 128:]
                return carry

            lax.fori_loop(0, PB // 8, body, 0)
        down = remote(rsp.at[ps, 0:HW], halo.at[1, ps], halo_send.at[1, b], halo_recv.at[1, b], at_z(-1))
        up = remote(rsp.at[ps, 2 * BS - HW:2 * BS], halo.at[0, ps], halo_send.at[0, b], halo_recv.at[0, b], at_z(1))
        down.start()
        up.start()
        halos += [(down, up)]

    total = jnp.zeros((2 * BS, 2 * BS + 2 * HW), jnp.float32)
    for b in range(BS // PB):
        for copy in halos[b]:
            copy.wait()
        left, wide = [], []
        for p in range(b * PB, (b + 1) * PB):
            left.append(occ[p])
            wide.append(jnp.concatenate([halo[0, p], rsp[p], halo[1, p]], axis=0))
        total = total + dot(jnp.concatenate(left, axis=1), jnp.concatenate(wide, axis=1), NT)

    shape = (2 * BS, 2 * BS + 2 * HW)
    at_row, at_col = lax.broadcasted_iota(jnp.int32, shape, 0), lax.broadcasted_iota(jnp.int32, shape, 1)
    outside = jnp.logical_or(
        jnp.logical_and(z == 0, at_col < HW), jnp.logical_and(z == Z - 1, at_col >= 2 * BS + HW)
    )
    band[...] = jnp.where(outside, 0.0, total)

    for xx in range(X):
        for c in range(2):
            first = c * BS + 3 * (xx // 2)
            shift = BS * c
            if xx % 2 == 0:
                one, two = band[pl.ds(first, 8, stride=6), :], band[pl.ds(first + 1, 8, stride=6), :]
                a, b, cut = (128 - shift) % 128, (80 - shift) % 128, 80
            else:
                one, two = band[pl.ds(first + 1, 8, stride=6), :], band[pl.ds(first + 2, 8, stride=6), :]
                a, b, cut = (128 - shift - 40) % 128, (40 - shift) % 128, 40
            one = pltpu.roll(one, a, 1) if a else one
            two = pltpu.roll(two, b, 1) if b else two
            parts[c, xx] = jnp.where(lane < cut, one, two)

    cross = remote(parts.at[other], cross_in, s1_send, s1_recv, sister)
    cross.start()
    cross.wait()
    rows_out[...] = (parts[core] + cross_in[...]).reshape(X * Y, 1, 128)
    copies = []
    for i, (dx, dy) in enumerate(plane):
        there = lax.rem(x + dx, X) * Y + lax.rem(y + dy, Y)
        copies.append(remote(rows_out.at[there], rows_in.at[i], s2_send.at[i], s2_recv.at[i], at_plane(dx, dy)))
        copies[-1].start()
    rows_in[X * Y - 1] = rows_out[x * Y + y]
    for copy in copies:
        copy.wait_recv()
    out_ref[...] = jnp.sum(rows_in[...], axis=0) * factor
    for copy in copies:
        copy.wait_send()


def local(tile_values, tile_owner, tile_block, coefficients):
    n_aux, n_ao = lax.axis_size("aux"), lax.axis_size("ao")
    Y, Z = n_aux // X, n_ao // 2
    count = tile_values.shape[0]
    held = coefficients.shape[0]
    factor = 1.0 / math.sqrt(256 * BS * n_aux)
    bf, f32 = jnp.bfloat16, jnp.float32
    dma = pltpu.SemaphoreType.DMA
    got = pl.pallas_call(
        functools.partial(kernel, Y, Z, factor),
        out_shape=jax.ShapeDtypeStruct((1, 128), f32),
        in_specs=[
            pl.BlockSpec(memory_space=pltpu.HBM),
            pl.BlockSpec(memory_space=pltpu.HBM),
            pl.BlockSpec(memory_space=pltpu.HBM),
            pl.BlockSpec(memory_space=pltpu.HBM),
        ],
        out_specs=pl.BlockSpec(memory_space=pltpu.VMEM),
        scratch_shapes=[
            pltpu.SMEM((count,), jnp.int32),
            pltpu.SMEM((count,), jnp.int32),
            pltpu.VMEM((count, BS, BS * BS), bf),
            pltpu.VMEM((768, 768), bf),
            pltpu.VMEM((2, BS, BS, 768), bf),
            pltpu.VMEM((n_ao * held, BS, 256), bf),
            pltpu.VMEM((2, 768, 256), bf),
            pltpu.VMEM((BS, 2 * BS, 128), bf),
            pltpu.VMEM((BS, 2 * BS, 128), bf),
            pltpu.VMEM((2, BS, HW, 128), bf),
            pltpu.VMEM((2 * BS, 2 * BS + 2 * HW), f32),
            pltpu.VMEM((2, X, 8, 128), f32),
            pltpu.VMEM((X, 8, 128), f32),
            pltpu.VMEM((X * Y, 1, 128), f32),
            pltpu.VMEM((X * Y, 1, 128), f32),
            pltpu.VMEM((2, 8, 128), jnp.int32),
            pltpu.SMEM((8, 128), jnp.int32),
            dma((2,)), dma, dma((2,)), dma((2,)), dma((2,)),
            dma((2, Z // 2, SUBS)), dma((2, Z // 2, SUBS)), dma((2, Z // 2, SUBS)), dma((2, Z // 2, SUBS)), dma((Y,)), dma((Y,)), dma((3,)), dma((3,)),
            dma, dma, dma,
            dma((2, BS // PB)), dma((2, BS // PB)),
            dma, dma, dma((X * Y,)), dma((X * Y,)),
        ],
        compiler_params=pltpu.CompilerParams(
            collective_id=0, has_side_effects=True, vmem_limit_bytes=60 * 1024 * 1024
        ),
        name="exchange",
    )(tile_owner.reshape(count), tile_block, tile_values, coefficients)
    return got[:, :BS * (BS + 2 * HW) // n_aux]


def solution(mesh):
    placed = (
        P(("aux", "ao"), None, None),
        P(("aux", "ao"), None),
        P(("aux", "ao")),
        P("ao", None, None),
    )
    return jax.shard_map(
        local, mesh=mesh, in_specs=placed, out_specs=P("ao", "aux"), check_vma=False
    )
```

```python
import functools
import math

import jax
import jax.numpy as jnp
from jax import lax
from jax.experimental import pallas as pl
from jax.experimental.pallas import tpu as pltpu
from jax.sharding import PartitionSpec as P

X = 4
BS = 48
HW = 16
PB = 16
SUBS = 4
NN = (((1,), (0,)), ((), ()))
NT = (((1,), (1,)), ((), ()))


def dot(a, b, dims):
    return lax.dot_general(a, b, dims, preferred_element_type=jnp.float32)


def kernel(
    Y, Z, factor,
    owner_hbm, block_hbm, tiles_ref, coef_ref, out_ref,
    owner_ref, block_ref,
    tiles, perm, tt, cg, picked, occ, rsp, halo, band, parts, cross_in, rows_out, rows_in, idx_v, idx_s,
    list_sem, tile_sem, coef_sem, sis_send, sis_recv, ring_send, ring_recv, side_send, side_recv, far_send, far_recv, tt_send, tt_recv,
    idx_send, idx_recv, idx_sem, halo_send, halo_recv, s1_send, s1_recv, s2_send, s2_recv, known,
):
    aux, ao = lax.axis_index("aux"), lax.axis_index("ao")
    y, x = aux // X, aux % X
    z, core = ao // 2, ao % 2
    other = 1 - core
    held = coef_ref.shape[0]
    per = 2 * held
    half = Z // 2
    plane = [(dx, dy) for dx in range(X) for dy in range(Y) if dx or dy]
    plane.sort(key=lambda at: -(min(at[0], X - at[0]) + min(at[1], Y - at[1])))

    def at_z(step):
        return {"aux": aux, "ao": lax.rem(z + step + Z, Z) * 2 + core}

    def at_plane(dx, dy):
        return {"aux": lax.rem(y + dy, Y) * X + lax.rem(x + dx, X), "ao": ao}

    sister = {"aux": aux, "ao": z * 2 + other}

    def remote(src, dst, send, recv, where):
        return pltpu.make_async_remote_copy(
            src_ref=src, dst_ref=dst, send_sem=send, recv_sem=recv,
            device_id=where, device_id_type=pl.DeviceIdType.MESH,
        )

    mine = ao * held
    local, swap = [], []
    for part in range(2):
        own = pl.ds(pl.multiple_of(part * 256 + core * 128, 128), 128)
        theirs = pl.ds(pl.multiple_of(part * 256 + other * 128, 128), 128)
        into = cg.at[pl.ds(mine, held), :, pl.ds(part * 128, 128)]
        local.append(pltpu.make_async_copy(coef_ref.at[:, :, own], into, coef_sem.at[part]))
        swap.append(remote(coef_ref.at[:, :, theirs], into, sis_send.at[part], sis_recv.at[part], sister))
    for copy in local:
        copy.start()

    tile_copy = pltpu.make_async_copy(tiles_ref, tiles, tile_sem)
    lists = [
        pltpu.make_async_copy(owner_hbm, owner_ref, list_sem.at[0]),
        pltpu.make_async_copy(block_hbm, block_ref, list_sem.at[1]),
    ]
    for copy in lists + [tile_copy]:
        copy.start()

    barrier = pltpu.get_barrier_semaphore()
    y_near, y_next = [at_plane(0, 1), at_plane(0, Y - 1)], [at_plane(0, 2), at_plane(0, Y - 2)]
    x_near = [at_plane(1, 0), at_plane(X - 1, 0)]
    y_ring = [at_plane(0, dy) for dy in range(1, Y)]
    peers = [sister, at_z(1), at_z(-1), at_z(half)] + x_near + y_near

    def tell(which, whom):
        for peer in whom:
            pl.semaphore_signal(known.at[which], inc=1, device_id=peer, device_id_type=pl.DeviceIdType.MESH)

    for peer in peers:
        pl.semaphore_signal(barrier, inc=1, device_id=peer, device_id_type=pl.DeviceIdType.MESH)
    pl.semaphore_wait(barrier, len(peers))
    for copy in swap:
        copy.start()

    size = held // SUBS
    odd = lax.rem(x + y, 2)

    def piece(slot, sub):
        part = lax.rem(sub // (SUBS // 2) + core, 2)
        start = part * held + odd * (held // 2) + sub % (SUBS // 2) * size
        return cg.at[pl.ds(lax.rem(slot + Z, Z) * per + start, size)]

    def beside(sub):
        step = (1 - 2 * odd) * (1 - 2 * (sub // 2))
        return at_plane(step + X, 0) if sub % 2 == 0 else at_plane(0, step + Y)

    started = []

    def go(copies):
        for copy in copies:
            copy.start()
        started.extend(copies)
        return copies

    def share(step, sub):
        slots = [z - step, z + step] if step < half else [z + step]
        refs = [piece(slot, sub) for slot in slots]
        return go([
            remote(ref, ref, side_send.at[i, step - 1, sub], side_recv.at[i, step - 1, sub], beside(sub))
            for i, ref in enumerate(refs)
        ])

    def hop(step, sub):
        refs = [piece(z - (step - 1), sub), piece(z + (step - 1), sub)]
        return go([
            remote(ref, ref, ring_send.at[i, step - 1, sub], ring_recv.at[i, step - 1, sub], at_z(1 - 2 * i))
            for i, ref in enumerate(refs)
        ])

    def fourth(slot):
        at = y // 2
        start = at // 2 * held + odd * (held // 2) + at % 2 * 2
        return cg.at[pl.ds(lax.rem(slot + Z, Z) * per + start, 2)]

    chains = []
    for copy in local:
        copy.wait()
    for sub in range(SUBS // 2):
        chains.append([hop(1, sub)])
    for copy in swap:
        copy.wait()
    far = remote(fourth(z), fourth(z), far_send.at[0], far_recv.at[0], at_z(half))
    far.start()
    for sub in range(SUBS // 2, SUBS):
        chains.append([hop(1, sub)])

    lane = lax.broadcasted_iota(jnp.int32, (8, 128), 1)
    listed = jnp.zeros((8, 128), jnp.int32)
    for copy in lists:
        copy.wait()
    for t in range(16):
        listed = jnp.where(lane == t, owner_ref[t] * held + block_ref[t], listed)
    idx_v[0] = listed
    idx_copy = remote(idx_v.at[0], idx_v.at[1], idx_send, idx_recv, sister)
    idx_copy.start()
    tell(0, y_near)
    tell(1, x_near)

    rows = lax.broadcasted_iota(jnp.int32, (768, 768), 0)
    want = (rows & 15) * BS + (rows >> 4)
    perm[...] = (lax.broadcasted_iota(jnp.int32, (768, 768), 1) == want).astype(jnp.bfloat16)

    def turn(part):
        rhs = tiles[:, :, part * 768:(part + 1) * 768].reshape(768, 768)

        def body(i, carry):
            start = pl.multiple_of(i * 256, 256)
            got = dot(perm[pl.ds(start, 256), :], rhs, NT).astype(jnp.bfloat16)
            tt[core, pl.ds(i * 16, 16), part * 16:(part + 1) * 16, :] = got.reshape(16, 16, 768)
            return carry

        lax.fori_loop(0, 3, body, 0)

    turned = []

    def turn_next():
        part = len(turned)
        turn(part)
        ref = tt.at[core, :, part * 16:(part + 1) * 16]
        turned.append(remote(ref, ref, tt_send.at[part], tt_recv.at[part], sister))
        turned[-1].start()

    sides, rounds = [], []
    pl.semaphore_wait(known.at[0], 2)
    tell(2, y_next)
    for step in range(2, half):
        for sub in range(SUBS):
            for copy in chains[sub][-1]:
                copy.wait_recv()
            chains[sub].append(hop(step, sub))
            sides += share(step - 1, sub)
        if step == 2:
            far.wait_recv()
            pl.semaphore_wait(known.at[2], 2)
            ref = fourth(z + half)
            for dy in (4, 2, 6):
                rounds.append(remote(ref, ref, far_send.at[dy], far_recv.at[dy], at_plane(0, dy)))
                rounds[-1].start()
            pl.semaphore_wait(known.at[1], 2)
            tell(3, y_ring)
            tile_copy.wait()
        turn_next()
    idx_copy.wait()
    fetch = pltpu.make_async_copy(idx_v.at[1], idx_s, idx_sem)
    fetch.start()
    turn_next()
    for copy in rounds:
        copy.wait_recv()
    for sub in range(SUBS):
        sides += share(half, sub)
    for sub in range(SUBS):
        for copy in chains[sub][-1]:
            copy.wait_recv()
        sides += share(half - 1, sub)
    fetch.wait()
    for copy in turned:
        copy.wait()
    for copy in sides:
        copy.wait_recv()
    for copy in started + rounds + [far]:
        copy.wait_send()

    for t in range(16):
        picked[core, t * BS:(t + 1) * BS, :] = cg[owner_ref[t] * held + block_ref[t]]
        picked[other, t * BS:(t + 1) * BS, :] = cg[idx_s[0, t]]

    halos = []
    for b in range(BS // PB):
        ps = pl.ds(b * PB, PB)
        for r in range(2):
            right = picked[r]

            got = dot(tt[r, ps].reshape(PB * BS, 768), right, NN).astype(jnp.bfloat16)
            got = got.reshape(PB, BS, 256)
            occ[ps, r * BS:(r + 1) * BS, :] = got[:, :, :128]
            rsp[ps, r * BS:(r + 1) * BS, :] = got[:, :, 128:]
        down = remote(rsp.at[ps, 0:HW], halo.at[1, ps], halo_send.at[1, b], halo_recv.at[1, b], at_z(-1))
        up = remote(rsp.at[ps, 2 * BS - HW:2 * BS], halo.at[0, ps], halo_send.at[0, b], halo_recv.at[0, b], at_z(1))
        down.start()
        up.start()
        halos += [(down, up)]

    total = jnp.zeros((2 * BS, 2 * BS + 2 * HW), jnp.float32)
    for b in range(BS // PB):
        for copy in halos[b]:
            copy.wait()
        left, wide = [], []
        for p in range(b * PB, (b + 1) * PB):
            left.append(occ[p])
            wide.append(jnp.concatenate([halo[0, p], rsp[p], halo[1, p]], axis=0))
        total = total + dot(jnp.concatenate(left, axis=1), jnp.concatenate(wide, axis=1), NT)

    shape = (2 * BS, 2 * BS + 2 * HW)
    at_row, at_col = lax.broadcasted_iota(jnp.int32, shape, 0), lax.broadcasted_iota(jnp.int32, shape, 1)
    outside = jnp.logical_or(
        jnp.logical_and(z == 0, at_col < HW), jnp.logical_and(z == Z - 1, at_col >= 2 * BS + HW)
    )
    band[...] = jnp.where(outside, 0.0, total)

    for xx in range(X):
        for c in range(2):
            first = c * BS + 3 * (xx // 2)
            shift = BS * c
            if xx % 2 == 0:
                one, two = band[pl.ds(first, 8, stride=6), :], band[pl.ds(first + 1, 8, stride=6), :]
                a, b, cut = (128 - shift) % 128, (80 - shift) % 128, 80
            else:
                one, two = band[pl.ds(first + 1, 8, stride=6), :], band[pl.ds(first + 2, 8, stride=6), :]
                a, b, cut = (128 - shift - 40) % 128, (40 - shift) % 128, 40
            one = pltpu.roll(one, a, 1) if a else one
            two = pltpu.roll(two, b, 1) if b else two
            parts[c, xx] = jnp.where(lane < cut, one, two)

    cross = remote(parts.at[other], cross_in, s1_send, s1_recv, sister)
    cross.start()
    cross.wait()
    pl.semaphore_wait(known.at[3], Y - 1)
    rows_out[...] = (parts[core] + cross_in[...]).reshape(X * Y, 1, 128)
    copies = []
    for i, (dx, dy) in enumerate(plane):
        there = lax.rem(x + dx, X) * Y + lax.rem(y + dy, Y)
        copies.append(remote(rows_out.at[there], rows_in.at[i], s2_send.at[i], s2_recv.at[i], at_plane(dx, dy)))
        copies[-1].start()
    rows_in[X * Y - 1] = rows_out[x * Y + y]
    for copy in copies:
        copy.wait_recv()
    out_ref[...] = jnp.sum(rows_in[...], axis=0) * factor
    for copy in copies:
        copy.wait_send()


def local(tile_values, tile_owner, tile_block, coefficients):
    n_aux, n_ao = lax.axis_size("aux"), lax.axis_size("ao")
    Y, Z = n_aux // X, n_ao // 2
    count = tile_values.shape[0]
    held = coefficients.shape[0]
    factor = 1.0 / math.sqrt(256 * BS * n_aux)
    bf, f32 = jnp.bfloat16, jnp.float32
    dma = pltpu.SemaphoreType.DMA
    got = pl.pallas_call(
        functools.partial(kernel, Y, Z, factor),
        out_shape=jax.ShapeDtypeStruct((1, 128), f32),
        in_specs=[
            pl.BlockSpec(memory_space=pltpu.HBM),
            pl.BlockSpec(memory_space=pltpu.HBM),
            pl.BlockSpec(memory_space=pltpu.HBM),
            pl.BlockSpec(memory_space=pltpu.HBM),
        ],
        out_specs=pl.BlockSpec(memory_space=pltpu.VMEM),
        scratch_shapes=[
            pltpu.SMEM((count,), jnp.int32),
            pltpu.SMEM((count,), jnp.int32),
            pltpu.VMEM((count, BS, BS * BS), bf),
            pltpu.VMEM((768, 768), bf),
            pltpu.VMEM((2, BS, BS, 768), bf),
            pltpu.VMEM((n_ao * held, BS, 256), bf),
            pltpu.VMEM((2, 768, 256), bf),
            pltpu.VMEM((BS, 2 * BS, 128), bf),
            pltpu.VMEM((BS, 2 * BS, 128), bf),
            pltpu.VMEM((2, BS, HW, 128), bf),
            pltpu.VMEM((2 * BS, 2 * BS + 2 * HW), f32),
            pltpu.VMEM((2, X, 8, 128), f32),
            pltpu.VMEM((X, 8, 128), f32),
            pltpu.VMEM((X * Y, 1, 128), f32),
            pltpu.VMEM((X * Y, 1, 128), f32),
            pltpu.VMEM((2, 8, 128), jnp.int32),
            pltpu.SMEM((8, 128), jnp.int32),
            dma((2,)), dma, dma((2,)), dma((2,)), dma((2,)),
            dma((2, Z // 2, SUBS)), dma((2, Z // 2, SUBS)), dma((2, Z // 2, SUBS)), dma((2, Z // 2, SUBS)), dma((Y,)), dma((Y,)), dma((3,)), dma((3,)),
            dma, dma, dma,
            dma((2, BS // PB)), dma((2, BS // PB)),
            dma, dma, dma((X * Y,)), dma((X * Y,)),
            pltpu.SemaphoreType.REGULAR((4,)),
        ],
        compiler_params=pltpu.CompilerParams(
            collective_id=0, has_side_effects=True, vmem_limit_bytes=60 * 1024 * 1024
        ),
        name="exchange",
    )(tile_owner.reshape(count), tile_block, tile_values, coefficients)
    return got[:, :BS * (BS + 2 * HW) // n_aux]


def solution(mesh):
    placed = (
        P(("aux", "ao"), None, None),
        P(("aux", "ao"), None),
        P(("aux", "ao")),
        P("ao", None, None),
    )
    return jax.shard_map(
        local, mesh=mesh, in_specs=placed, out_specs=P("ao", "aux"), check_vma=False
    )
```

```python
import functools
import math

import jax
import jax.numpy as jnp
from jax import lax
from jax.experimental import pallas as pl
from jax.experimental.pallas import tpu as pltpu
from jax.sharding import PartitionSpec as P

X = 4
BS = 48
HW = 16
PB = 16
SUBS = 4
NN = (((1,), (0,)), ((), ()))
NT = (((1,), (1,)), ((), ()))


def dot(a, b, dims):
    return lax.dot_general(a, b, dims, preferred_element_type=jnp.float32)


def kernel(
    Y, Z, factor,
    owner_hbm, block_hbm, tiles_ref, coef_ref, out_ref,
    owner_ref, block_ref,
    tiles, perm, tt, cg, picked, occ, rsp, halo, band, parts, cross_in, rows_out, rows_in, idx_v, idx_s,
    list_sem, tile_sem, coef_sem, sis_send, sis_recv, ring_send, ring_recv, side_send, side_recv, far_send, far_recv, tt_send, tt_recv,
    idx_send, idx_recv, idx_sem, halo_send, halo_recv, s1_send, s1_recv, s2_send, s2_recv, known,
):
    aux, ao = lax.axis_index("aux"), lax.axis_index("ao")
    y, x = aux // X, aux % X
    z, core = ao // 2, ao % 2
    other = 1 - core
    held = coef_ref.shape[0]
    per = 2 * held
    half = Z // 2
    plane = [(dx, dy) for dx in range(X) for dy in range(Y) if dx or dy]
    plane.sort(key=lambda at: -(min(at[0], X - at[0]) + min(at[1], Y - at[1])))

    def at_z(step):
        return {"aux": aux, "ao": lax.rem(z + step + Z, Z) * 2 + core}

    def at_plane(dx, dy):
        return {"aux": lax.rem(y + dy, Y) * X + lax.rem(x + dx, X), "ao": ao}

    sister = {"aux": aux, "ao": z * 2 + other}

    def remote(src, dst, send, recv, where):
        return pltpu.make_async_remote_copy(
            src_ref=src, dst_ref=dst, send_sem=send, recv_sem=recv,
            device_id=where, device_id_type=pl.DeviceIdType.MESH,
        )

    mine = ao * held
    local, swap = [], []
    for part in range(2):
        own = pl.ds(pl.multiple_of(part * 256 + core * 128, 128), 128)
        theirs = pl.ds(pl.multiple_of(part * 256 + other * 128, 128), 128)
        into = cg.at[pl.ds(mine, held), :, pl.ds(part * 128, 128)]
        local.append(pltpu.make_async_copy(coef_ref.at[:, :, own], into, coef_sem.at[part]))
        swap.append(remote(coef_ref.at[:, :, theirs], into, sis_send.at[part], sis_recv.at[part], sister))
    for copy in local:
        copy.start()

    tile_copy = pltpu.make_async_copy(tiles_ref, tiles, tile_sem)
    lists = [
        pltpu.make_async_copy(owner_hbm, owner_ref, list_sem.at[0]),
        pltpu.make_async_copy(block_hbm, block_ref, list_sem.at[1]),
    ]
    for copy in lists + [tile_copy]:
        copy.start()

    barrier = pltpu.get_barrier_semaphore()
    y_near, y_next = [at_plane(0, 1), at_plane(0, Y - 1)], [at_plane(0, 2), at_plane(0, Y - 2)]
    x_near = [at_plane(1, 0), at_plane(X - 1, 0)]
    y_ring = [at_plane(0, dy) for dy in range(1, Y)]
    peers = [sister, at_z(1), at_z(-1), at_z(half)] + x_near + y_near

    def tell(which, whom):
        for peer in whom:
            pl.semaphore_signal(known.at[which], inc=1, device_id=peer, device_id_type=pl.DeviceIdType.MESH)

    for peer in peers:
        pl.semaphore_signal(barrier, inc=1, device_id=peer, device_id_type=pl.DeviceIdType.MESH)
    pl.semaphore_wait(barrier, len(peers))
    for copy in swap:
        copy.start()

    size = held // SUBS
    odd = lax.rem(x + y, 2)

    def piece(slot, sub):
        part = lax.rem(sub // (SUBS // 2) + core, 2)
        start = part * held + odd * (held // 2) + sub % (SUBS // 2) * size
        return cg.at[pl.ds(lax.rem(slot + Z, Z) * per + start, size)]

    def beside(sub):
        step = (1 - 2 * odd) * (1 - 2 * (sub // 2))
        return at_plane(step + X, 0) if sub % 2 == 0 else at_plane(0, step + Y)

    started = []

    def go(copies):
        for copy in copies:
            copy.start()
        started.extend(copies)
        return copies

    def share(step, sub):
        slots = [z - step, z + step] if step < half else [z + step]
        refs = [piece(slot, sub) for slot in slots]
        return go([
            remote(ref, ref, side_send.at[i, step - 1, sub], side_recv.at[i, step - 1, sub], beside(sub))
            for i, ref in enumerate(refs)
        ])

    def hop(step, sub):
        refs = [piece(z - (step - 1), sub), piece(z + (step - 1), sub)]
        return go([
            remote(ref, ref, ring_send.at[i, step - 1, sub], ring_recv.at[i, step - 1, sub], at_z(1 - 2 * i))
            for i, ref in enumerate(refs)
        ])

    def fourth(slot):
        at = y // 2
        start = at // 2 * held + odd * (held // 2) + at % 2 * 2
        return cg.at[pl.ds(lax.rem(slot + Z, Z) * per + start, 2)]

    chains = []
    for copy in local:
        copy.wait()
    for sub in range(SUBS // 2):
        chains.append([hop(1, sub)])
    for copy in swap:
        copy.wait_recv()
    far = remote(fourth(z), fourth(z), far_send.at[0], far_recv.at[0], at_z(half))
    far.start()
    for sub in range(SUBS // 2, SUBS):
        chains.append([hop(1, sub)])

    lane = lax.broadcasted_iota(jnp.int32, (8, 128), 1)
    listed = jnp.zeros((8, 128), jnp.int32)
    for copy in lists:
        copy.wait()
    for t in range(16):
        listed = jnp.where(lane == t, owner_ref[t] * held + block_ref[t], listed)
    idx_v[0] = listed
    idx_copy = remote(idx_v.at[0], idx_v.at[1], idx_send, idx_recv, sister)
    idx_copy.start()
    tell(0, y_near)
    tell(1, x_near)

    rows = lax.broadcasted_iota(jnp.int32, (768, 768), 0)
    want = (rows & 15) * BS + (rows >> 4)
    perm[...] = (lax.broadcasted_iota(jnp.int32, (768, 768), 1) == want).astype(jnp.bfloat16)

    def turn(part):
        rhs = tiles[:, :, part * 768:(part + 1) * 768].reshape(768, 768)

        def body(i, carry):
            start = pl.multiple_of(i * 256, 256)
            got = dot(perm[pl.ds(start, 256), :], rhs, NT).astype(jnp.bfloat16)
            tt[core, pl.ds(i * 16, 16), part * 16:(part + 1) * 16, :] = got.reshape(16, 16, 768)
            return carry

        lax.fori_loop(0, 3, body, 0)

    turned = []

    def turn_next():
        part = len(turned)
        turn(part)
        ref = tt.at[core, :, part * 16:(part + 1) * 16]
        turned.append(remote(ref, ref, tt_send.at[part], tt_recv.at[part], sister))
        turned[-1].start()

    sides, rounds = [], []
    pl.semaphore_wait(known.at[0], 2)
    tell(2, y_next)
    for step in range(2, half):
        for sub in range(SUBS):
            for copy in chains[sub][-1]:
                copy.wait_recv()
            chains[sub].append(hop(step, sub))
            sides += share(step - 1, sub)
        if step == 2:
            far.wait_recv()
            pl.semaphore_wait(known.at[2], 2)
            ref = fourth(z + half)
            for dy in (4, 2, 6):
                rounds.append(remote(ref, ref, far_send.at[dy], far_recv.at[dy], at_plane(0, dy)))
                rounds[-1].start()
            pl.semaphore_wait(known.at[1], 2)
            tell(3, y_ring)
            tile_copy.wait()
        turn_next()
    idx_copy.wait_recv()
    fetch = pltpu.make_async_copy(idx_v.at[1], idx_s, idx_sem)
    fetch.start()
    turn_next()
    for copy in rounds:
        copy.wait_recv()
    for sub in range(SUBS):
        sides += share(half, sub)
    for sub in range(SUBS):
        for copy in chains[sub][-1]:
            copy.wait_recv()
        sides += share(half - 1, sub)
    fetch.wait()
    for copy in turned:
        copy.wait_recv()
    for copy in sides:
        copy.wait_recv()

    for t in range(16):
        picked[core, t * BS:(t + 1) * BS, :] = cg[owner_ref[t] * held + block_ref[t]]
        picked[other, t * BS:(t + 1) * BS, :] = cg[idx_s[0, t]]

    halos = []
    for b in range(BS // PB):
        ps = pl.ds(b * PB, PB)
        for r in range(2):
            right = picked[r]

            got = dot(tt[r, ps].reshape(PB * BS, 768), right, NN).astype(jnp.bfloat16)
            got = got.reshape(PB, BS, 256)
            occ[ps, r * BS:(r + 1) * BS, :] = got[:, :, :128]
            rsp[ps, r * BS:(r + 1) * BS, :] = got[:, :, 128:]
        down = remote(rsp.at[ps, 0:HW], halo.at[1, ps], halo_send.at[1, b], halo_recv.at[1, b], at_z(-1))
        up = remote(rsp.at[ps, 2 * BS - HW:2 * BS], halo.at[0, ps], halo_send.at[0, b], halo_recv.at[0, b], at_z(1))
        down.start()
        up.start()
        halos += [(down, up)]

    total = jnp.zeros((2 * BS, 2 * BS + 2 * HW), jnp.float32)
    for b in range(BS // PB):
        for copy in halos[b]:
            copy.wait_recv()
        left, wide = [], []
        for p in range(b * PB, (b + 1) * PB):
            left.append(occ[p])
            wide.append(jnp.concatenate([halo[0, p], rsp[p], halo[1, p]], axis=0))
        total = total + dot(jnp.concatenate(left, axis=1), jnp.concatenate(wide, axis=1), NT)

    shape = (2 * BS, 2 * BS + 2 * HW)
    at_row, at_col = lax.broadcasted_iota(jnp.int32, shape, 0), lax.broadcasted_iota(jnp.int32, shape, 1)
    outside = jnp.logical_or(
        jnp.logical_and(z == 0, at_col < HW), jnp.logical_and(z == Z - 1, at_col >= 2 * BS + HW)
    )
    band[...] = jnp.where(outside, 0.0, total)

    for xx in range(X):
        for c in range(2):
            first = c * BS + 3 * (xx // 2)
            shift = BS * c
            if xx % 2 == 0:
                one, two = band[pl.ds(first, 8, stride=6), :], band[pl.ds(first + 1, 8, stride=6), :]
                a, b, cut = (128 - shift) % 128, (80 - shift) % 128, 80
            else:
                one, two = band[pl.ds(first + 1, 8, stride=6), :], band[pl.ds(first + 2, 8, stride=6), :]
                a, b, cut = (128 - shift - 40) % 128, (40 - shift) % 128, 40
            one = pltpu.roll(one, a, 1) if a else one
            two = pltpu.roll(two, b, 1) if b else two
            parts[c, xx] = jnp.where(lane < cut, one, two)

    cross = remote(parts.at[other], cross_in, s1_send, s1_recv, sister)
    cross.start()
    cross.wait_recv()
    pl.semaphore_wait(known.at[3], Y - 1)
    rows_out[...] = (parts[core] + cross_in[...]).reshape(X * Y, 1, 128)
    copies = []
    for i, (dx, dy) in enumerate(plane):
        there = lax.rem(x + dx, X) * Y + lax.rem(y + dy, Y)
        copies.append(remote(rows_out.at[there], rows_in.at[i], s2_send.at[i], s2_recv.at[i], at_plane(dx, dy)))
        copies[-1].start()
    rows_in[X * Y - 1] = rows_out[x * Y + y]
    for copy in copies:
        copy.wait_recv()
    out_ref[...] = jnp.sum(rows_in[...], axis=0) * factor
    for pair in halos:
        copies += pair
    for copy in swap + turned + started + rounds + copies + [idx_copy, far, cross]:
        copy.wait_send()


def local(tile_values, tile_owner, tile_block, coefficients):
    n_aux, n_ao = lax.axis_size("aux"), lax.axis_size("ao")
    Y, Z = n_aux // X, n_ao // 2
    count = tile_values.shape[0]
    held = coefficients.shape[0]
    factor = 1.0 / math.sqrt(256 * BS * n_aux)
    bf, f32 = jnp.bfloat16, jnp.float32
    dma = pltpu.SemaphoreType.DMA
    got = pl.pallas_call(
        functools.partial(kernel, Y, Z, factor),
        out_shape=jax.ShapeDtypeStruct((1, 128), f32),
        in_specs=[
            pl.BlockSpec(memory_space=pltpu.HBM),
            pl.BlockSpec(memory_space=pltpu.HBM),
            pl.BlockSpec(memory_space=pltpu.HBM),
            pl.BlockSpec(memory_space=pltpu.HBM),
        ],
        out_specs=pl.BlockSpec(memory_space=pltpu.VMEM),
        scratch_shapes=[
            pltpu.SMEM((count,), jnp.int32),
            pltpu.SMEM((count,), jnp.int32),
            pltpu.VMEM((count, BS, BS * BS), bf),
            pltpu.VMEM((768, 768), bf),
            pltpu.VMEM((2, BS, BS, 768), bf),
            pltpu.VMEM((n_ao * held, BS, 256), bf),
            pltpu.VMEM((2, 768, 256), bf),
            pltpu.VMEM((BS, 2 * BS, 128), bf),
            pltpu.VMEM((BS, 2 * BS, 128), bf),
            pltpu.VMEM((2, BS, HW, 128), bf),
            pltpu.VMEM((2 * BS, 2 * BS + 2 * HW), f32),
            pltpu.VMEM((2, X, 8, 128), f32),
            pltpu.VMEM((X, 8, 128), f32),
            pltpu.VMEM((X * Y, 1, 128), f32),
            pltpu.VMEM((X * Y, 1, 128), f32),
            pltpu.VMEM((2, 8, 128), jnp.int32),
            pltpu.SMEM((8, 128), jnp.int32),
            dma((2,)), dma, dma((2,)), dma((2,)), dma((2,)),
            dma((2, Z // 2, SUBS)), dma((2, Z // 2, SUBS)), dma((2, Z // 2, SUBS)), dma((2, Z // 2, SUBS)), dma((Y,)), dma((Y,)), dma((3,)), dma((3,)),
            dma, dma, dma,
            dma((2, BS // PB)), dma((2, BS // PB)),
            dma, dma, dma((X * Y,)), dma((X * Y,)),
            pltpu.SemaphoreType.REGULAR((4,)),
        ],
        compiler_params=pltpu.CompilerParams(
            collective_id=0, has_side_effects=True, vmem_limit_bytes=60 * 1024 * 1024
        ),
        name="exchange",
    )(tile_owner.reshape(count), tile_block, tile_values, coefficients)
    return got[:, :BS * (BS + 2 * HW) // n_aux]


def solution(mesh):
    placed = (
        P(("aux", "ao"), None, None),
        P(("aux", "ao"), None),
        P(("aux", "ao")),
        P("ao", None, None),
    )
    return jax.shard_map(
        local, mesh=mesh, in_specs=placed, out_specs=P("ao", "aux"), check_vma=False
    )
```

```python
import functools
import math

import jax
import jax.numpy as jnp
from jax import lax
from jax.experimental import pallas as pl
from jax.experimental.pallas import tpu as pltpu
from jax.sharding import PartitionSpec as P

X = 4
BS = 48
HW = 16
PB = 8
SUBS = 4
NN = (((1,), (0,)), ((), ()))
NT = (((1,), (1,)), ((), ()))


def dot(a, b, dims):
    return lax.dot_general(a, b, dims, preferred_element_type=jnp.float32)


def kernel(
    Y, Z, factor,
    owner_hbm, block_hbm, tiles_ref, coef_ref, out_ref,
    owner_ref, block_ref,
    tiles, perm, tt, cg, picked, occ, rsp, halo, band, parts, cross_in, rows_out, rows_in, idx_v, idx_s,
    list_sem, tile_sem, coef_sem, sis_send, sis_recv, ring_send, ring_recv, side_send, side_recv, far_send, far_recv, tt_send, tt_recv,
    idx_send, idx_recv, idx_sem, halo_send, halo_recv, s1_send, s1_recv, s2_send, s2_recv, known,
):
    aux, ao = lax.axis_index("aux"), lax.axis_index("ao")
    y, x = aux // X, aux % X
    z, core = ao // 2, ao % 2
    other = 1 - core
    held = coef_ref.shape[0]
    per = 2 * held
    half = Z // 2
    plane = [(dx, dy) for dx in range(X) for dy in range(Y) if dx or dy]
    plane.sort(key=lambda at: -(min(at[0], X - at[0]) + min(at[1], Y - at[1])))

    def at_z(step):
        return {"aux": aux, "ao": lax.rem(z + step + Z, Z) * 2 + core}

    def at_plane(dx, dy):
        return {"aux": lax.rem(y + dy, Y) * X + lax.rem(x + dx, X), "ao": ao}

    sister = {"aux": aux, "ao": z * 2 + other}

    def remote(src, dst, send, recv, where):
        return pltpu.make_async_remote_copy(
            src_ref=src, dst_ref=dst, send_sem=send, recv_sem=recv,
            device_id=where, device_id_type=pl.DeviceIdType.MESH,
        )

    mine = ao * held
    local, swap = [], []
    for part in range(2):
        own = pl.ds(pl.multiple_of(part * 256 + core * 128, 128), 128)
        theirs = pl.ds(pl.multiple_of(part * 256 + other * 128, 128), 128)
        into = cg.at[pl.ds(mine, held), :, pl.ds(part * 128, 128)]
        local.append(pltpu.make_async_copy(coef_ref.at[:, :, own], into, coef_sem.at[part]))
        swap.append(remote(coef_ref.at[:, :, theirs], into, sis_send.at[part], sis_recv.at[part], sister))
    for copy in local:
        copy.start()

    tile_copy = pltpu.make_async_copy(tiles_ref, tiles, tile_sem)
    lists = [
        pltpu.make_async_copy(owner_hbm, owner_ref, list_sem.at[0]),
        pltpu.make_async_copy(block_hbm, block_ref, list_sem.at[1]),
    ]
    for copy in lists + [tile_copy]:
        copy.start()

    barrier = pltpu.get_barrier_semaphore()
    y_near, y_next = [at_plane(0, 1), at_plane(0, Y - 1)], [at_plane(0, 2), at_plane(0, Y - 2)]
    x_near = [at_plane(1, 0), at_plane(X - 1, 0)]
    y_ring = [at_plane(0, dy) for dy in range(1, Y)]
    peers = [sister, at_z(1), at_z(-1), at_z(half)] + x_near + y_near

    def tell(which, whom):
        for peer in whom:
            pl.semaphore_signal(known.at[which], inc=1, device_id=peer, device_id_type=pl.DeviceIdType.MESH)

    for peer in peers:
        pl.semaphore_signal(barrier, inc=1, device_id=peer, device_id_type=pl.DeviceIdType.MESH)
    pl.semaphore_wait(barrier, len(peers))
    for copy in swap:
        copy.start()

    size = held // SUBS
    odd = lax.rem(x + y, 2)

    def piece(slot, sub):
        part = lax.rem(sub // (SUBS // 2) + core, 2)
        start = part * held + odd * (held // 2) + sub % (SUBS // 2) * size
        return cg.at[pl.ds(lax.rem(slot + Z, Z) * per + start, size)]

    def beside(sub):
        step = (1 - 2 * odd) * (1 - 2 * (sub // 2))
        return at_plane(step + X, 0) if sub % 2 == 0 else at_plane(0, step + Y)

    started = []

    def go(copies):
        for copy in copies:
            copy.start()
        started.extend(copies)
        return copies

    def share(step, sub):
        slots = [z - step, z + step] if step < half else [z + step]
        refs = [piece(slot, sub) for slot in slots]
        return go([
            remote(ref, ref, side_send.at[i, step - 1, sub], side_recv.at[i, step - 1, sub], beside(sub))
            for i, ref in enumerate(refs)
        ])

    def hop(step, sub):
        refs = [piece(z - (step - 1), sub), piece(z + (step - 1), sub)]
        return go([
            remote(ref, ref, ring_send.at[i, step - 1, sub], ring_recv.at[i, step - 1, sub], at_z(1 - 2 * i))
            for i, ref in enumerate(refs)
        ])

    def fourth(slot):
        at = y // 2
        start = at // 2 * held + odd * (held // 2) + at % 2 * 2
        return cg.at[pl.ds(lax.rem(slot + Z, Z) * per + start, 2)]

    chains = []
    for copy in local:
        copy.wait()
    for sub in range(SUBS // 2):
        chains.append([hop(1, sub)])
    for copy in swap:
        copy.wait_recv()
    far = remote(fourth(z), fourth(z), far_send.at[0], far_recv.at[0], at_z(half))
    far.start()
    for sub in range(SUBS // 2, SUBS):
        chains.append([hop(1, sub)])

    lane = lax.broadcasted_iota(jnp.int32, (8, 128), 1)
    listed = jnp.zeros((8, 128), jnp.int32)
    for copy in lists:
        copy.wait()
    for t in range(16):
        listed = jnp.where(lane == t, owner_ref[t] * held + block_ref[t], listed)
    idx_v[0] = listed
    idx_copy = remote(idx_v.at[0], idx_v.at[1], idx_send, idx_recv, sister)
    idx_copy.start()
    tell(0, y_near)
    tell(1, x_near)

    rows = lax.broadcasted_iota(jnp.int32, (768, 768), 0)
    want = (rows & 15) * BS + (rows >> 4)
    perm[...] = (lax.broadcasted_iota(jnp.int32, (768, 768), 1) == want).astype(jnp.bfloat16)

    def turn(part):
        rhs = tiles[:, :, part * 768:(part + 1) * 768].reshape(768, 768)

        def body(i, carry):
            start = pl.multiple_of(i * 256, 256)
            got = dot(perm[pl.ds(start, 256), :], rhs, NT).astype(jnp.bfloat16)
            tt[core, pl.ds(i * 16, 16), part * 16:(part + 1) * 16, :] = got.reshape(16, 16, 768)
            return carry

        lax.fori_loop(0, 3, body, 0)

    turned = []

    def turn_next():
        part = len(turned)
        turn(part)
        ref = tt.at[core, :, part * 16:(part + 1) * 16]
        turned.append(remote(ref, ref, tt_send.at[part], tt_recv.at[part], sister))
        turned[-1].start()

    sides, rounds = [], []
    pl.semaphore_wait(known.at[0], 2)
    tell(2, y_next)
    for step in range(2, half):
        for sub in range(SUBS):
            for copy in chains[sub][-1]:
                copy.wait_recv()
            chains[sub].append(hop(step, sub))
            sides += share(step - 1, sub)
        if step == 2:
            far.wait_recv()
            pl.semaphore_wait(known.at[2], 2)
            ref = fourth(z + half)
            for dy in (4, 2, 6):
                rounds.append(remote(ref, ref, far_send.at[dy], far_recv.at[dy], at_plane(0, dy)))
                rounds[-1].start()
            pl.semaphore_wait(known.at[1], 2)
            tell(3, y_ring)
            tile_copy.wait()
        turn_next()
    idx_copy.wait_recv()
    fetch = pltpu.make_async_copy(idx_v.at[1], idx_s, idx_sem)
    fetch.start()
    turn_next()
    for copy in rounds:
        copy.wait_recv()
    for sub in range(SUBS):
        sides += share(half, sub)
    for sub in range(SUBS):
        for copy in chains[sub][-1]:
            copy.wait_recv()
        sides += share(half - 1, sub)
    fetch.wait()
    for copy in turned:
        copy.wait_recv()
    for copy in sides:
        copy.wait_recv()

    for t in range(16):
        picked[core, t * BS:(t + 1) * BS, :] = cg[owner_ref[t] * held + block_ref[t]]
        picked[other, t * BS:(t + 1) * BS, :] = cg[idx_s[0, t]]

    halos = []
    for b in range(BS // PB):
        ps = pl.ds(b * PB, PB)
        for r in range(2):
            right = picked[r]

            got = dot(tt[r, ps].reshape(PB * BS, 768), right, NN).astype(jnp.bfloat16)
            got = got.reshape(PB, BS, 256)
            occ[ps, r * BS:(r + 1) * BS, :] = got[:, :, :128]
            rsp[ps, r * BS:(r + 1) * BS, :] = got[:, :, 128:]
        down = remote(rsp.at[ps, 0:HW], halo.at[1, ps], halo_send.at[1, b], halo_recv.at[1, b], at_z(-1))
        up = remote(rsp.at[ps, 2 * BS - HW:2 * BS], halo.at[0, ps], halo_send.at[0, b], halo_recv.at[0, b], at_z(1))
        down.start()
        up.start()
        halos += [(down, up)]

    total = jnp.zeros((2 * BS, 2 * BS + 2 * HW), jnp.float32)
    for b in range(BS // PB):
        for copy in halos[b]:
            copy.wait_recv()
        left, wide = [], []
        for p in range(b * PB, (b + 1) * PB):
            left.append(occ[p])
            wide.append(jnp.concatenate([halo[0, p], rsp[p], halo[1, p]], axis=0))
        total = total + dot(jnp.concatenate(left, axis=1), jnp.concatenate(wide, axis=1), NT)

    shape = (2 * BS, 2 * BS + 2 * HW)
    at_row, at_col = lax.broadcasted_iota(jnp.int32, shape, 0), lax.broadcasted_iota(jnp.int32, shape, 1)
    outside = jnp.logical_or(
        jnp.logical_and(z == 0, at_col < HW), jnp.logical_and(z == Z - 1, at_col >= 2 * BS + HW)
    )
    band[...] = jnp.where(outside, 0.0, total)

    for xx in range(X):
        for c in range(2):
            first = c * BS + 3 * (xx // 2)
            shift = BS * c
            if xx % 2 == 0:
                one, two = band[pl.ds(first, 8, stride=6), :], band[pl.ds(first + 1, 8, stride=6), :]
                a, b, cut = (128 - shift) % 128, (80 - shift) % 128, 80
            else:
                one, two = band[pl.ds(first + 1, 8, stride=6), :], band[pl.ds(first + 2, 8, stride=6), :]
                a, b, cut = (128 - shift - 40) % 128, (40 - shift) % 128, 40
            one = pltpu.roll(one, a, 1) if a else one
            two = pltpu.roll(two, b, 1) if b else two
            parts[c, xx] = jnp.where(lane < cut, one, two)

    cross = remote(parts.at[other], cross_in, s1_send, s1_recv, sister)
    cross.start()
    cross.wait_recv()
    pl.semaphore_wait(known.at[3], Y - 1)
    rows_out[...] = (parts[core] + cross_in[...]).reshape(X * Y, 1, 128)
    copies = []
    for i, (dx, dy) in enumerate(plane):
        there = lax.rem(x + dx, X) * Y + lax.rem(y + dy, Y)
        copies.append(remote(rows_out.at[there], rows_in.at[i], s2_send.at[i], s2_recv.at[i], at_plane(dx, dy)))
        copies[-1].start()
    rows_in[X * Y - 1] = rows_out[x * Y + y]
    for copy in copies:
        copy.wait_recv()
    out_ref[...] = jnp.sum(rows_in[...], axis=0) * factor
    for pair in halos:
        copies += pair
    for copy in swap + turned + started + rounds + copies + [idx_copy, far, cross]:
        copy.wait_send()


def local(tile_values, tile_owner, tile_block, coefficients):
    n_aux, n_ao = lax.axis_size("aux"), lax.axis_size("ao")
    Y, Z = n_aux // X, n_ao // 2
    count = tile_values.shape[0]
    held = coefficients.shape[0]
    factor = 1.0 / math.sqrt(256 * BS * n_aux)
    bf, f32 = jnp.bfloat16, jnp.float32
    dma = pltpu.SemaphoreType.DMA
    got = pl.pallas_call(
        functools.partial(kernel, Y, Z, factor),
        out_shape=jax.ShapeDtypeStruct((1, 128), f32),
        in_specs=[
            pl.BlockSpec(memory_space=pltpu.HBM),
            pl.BlockSpec(memory_space=pltpu.HBM),
            pl.BlockSpec(memory_space=pltpu.HBM),
            pl.BlockSpec(memory_space=pltpu.HBM),
        ],
        out_specs=pl.BlockSpec(memory_space=pltpu.VMEM),
        scratch_shapes=[
            pltpu.SMEM((count,), jnp.int32),
            pltpu.SMEM((count,), jnp.int32),
            pltpu.VMEM((count, BS, BS * BS), bf),
            pltpu.VMEM((768, 768), bf),
            pltpu.VMEM((2, BS, BS, 768), bf),
            pltpu.VMEM((n_ao * held, BS, 256), bf),
            pltpu.VMEM((2, 768, 256), bf),
            pltpu.VMEM((BS, 2 * BS, 128), bf),
            pltpu.VMEM((BS, 2 * BS, 128), bf),
            pltpu.VMEM((2, BS, HW, 128), bf),
            pltpu.VMEM((2 * BS, 2 * BS + 2 * HW), f32),
            pltpu.VMEM((2, X, 8, 128), f32),
            pltpu.VMEM((X, 8, 128), f32),
            pltpu.VMEM((X * Y, 1, 128), f32),
            pltpu.VMEM((X * Y, 1, 128), f32),
            pltpu.VMEM((2, 8, 128), jnp.int32),
            pltpu.SMEM((8, 128), jnp.int32),
            dma((2,)), dma, dma((2,)), dma((2,)), dma((2,)),
            dma((2, Z // 2, SUBS)), dma((2, Z // 2, SUBS)), dma((2, Z // 2, SUBS)), dma((2, Z // 2, SUBS)), dma((Y,)), dma((Y,)), dma((3,)), dma((3,)),
            dma, dma, dma,
            dma((2, BS // PB)), dma((2, BS // PB)),
            dma, dma, dma((X * Y,)), dma((X * Y,)),
            pltpu.SemaphoreType.REGULAR((4,)),
        ],
        compiler_params=pltpu.CompilerParams(
            collective_id=0, has_side_effects=True, vmem_limit_bytes=60 * 1024 * 1024
        ),
        name="exchange",
    )(tile_owner.reshape(count), tile_block, tile_values, coefficients)
    return got[:, :BS * (BS + 2 * HW) // n_aux]


def solution(mesh):
    placed = (
        P(("aux", "ao"), None, None),
        P(("aux", "ao"), None),
        P(("aux", "ao")),
        P("ao", None, None),
    )
    return jax.shard_map(
        local, mesh=mesh, in_specs=placed, out_specs=P("ao", "aux"), check_vma=False
    )
```

```python
import functools
import math

import jax
import jax.numpy as jnp
from jax import lax
from jax.experimental import pallas as pl
from jax.experimental.pallas import tpu as pltpu
from jax.sharding import PartitionSpec as P

X = 4
BS = 48
HW = 16
PB = 8
SUBS = 4
NN = (((1,), (0,)), ((), ()))
NT = (((1,), (1,)), ((), ()))


def dot(a, b, dims):
    return lax.dot_general(a, b, dims, preferred_element_type=jnp.float32)


def kernel(
    Y, Z, factor,
    owner_hbm, block_hbm, tiles_ref, coef_ref, out_ref,
    owner_ref, block_ref,
    tiles, perm, tt, cg, picked, occ, rsp, halo, band, parts, cross_in, rows_out, rows_in, idx_v, idx_s,
    list_sem, tile_sem, coef_sem, sis_send, sis_recv, ring_send, ring_recv, side_send, side_recv, far_send, far_recv, tt_send, tt_recv,
    idx_send, idx_recv, idx_sem, halo_send, halo_recv, s1_send, s1_recv, s2_send, s2_recv, known,
):
    aux, ao = lax.axis_index("aux"), lax.axis_index("ao")
    y, x = aux // X, aux % X
    z, core = ao // 2, ao % 2
    other = 1 - core
    held = coef_ref.shape[0]
    per = 2 * held
    half = Z // 2
    plane = [(dx, dy) for dx in range(X) for dy in range(Y) if dx or dy]
    plane.sort(key=lambda at: -(min(at[0], X - at[0]) + min(at[1], Y - at[1])))

    def at_z(step):
        return {"aux": aux, "ao": lax.rem(z + step + Z, Z) * 2 + core}

    def at_plane(dx, dy):
        return {"aux": lax.rem(y + dy, Y) * X + lax.rem(x + dx, X), "ao": ao}

    sister = {"aux": aux, "ao": z * 2 + other}

    def remote(src, dst, send, recv, where):
        return pltpu.make_async_remote_copy(
            src_ref=src, dst_ref=dst, send_sem=send, recv_sem=recv,
            device_id=where, device_id_type=pl.DeviceIdType.MESH,
        )

    mine = ao * held
    local, swap = [], []
    for part in range(2):
        own = pl.ds(pl.multiple_of(part * 256 + core * 128, 128), 128)
        theirs = pl.ds(pl.multiple_of(part * 256 + other * 128, 128), 128)
        into = cg.at[pl.ds(mine, held), :, pl.ds(part * 128, 128)]
        local.append(pltpu.make_async_copy(coef_ref.at[:, :, own], into, coef_sem.at[part]))
        swap.append(remote(coef_ref.at[:, :, theirs], into, sis_send.at[part], sis_recv.at[part], sister))
    for copy in local:
        copy.start()

    tile_copy = pltpu.make_async_copy(tiles_ref, tiles, tile_sem)
    lists = [
        pltpu.make_async_copy(owner_hbm, owner_ref, list_sem.at[0]),
        pltpu.make_async_copy(block_hbm, block_ref, list_sem.at[1]),
    ]
    for copy in lists + [tile_copy]:
        copy.start()

    barrier = pltpu.get_barrier_semaphore()
    y_near, y_next = [at_plane(0, 1), at_plane(0, Y - 1)], [at_plane(0, 2), at_plane(0, Y - 2)]
    x_near = [at_plane(1, 0), at_plane(X - 1, 0)]
    y_ring = [at_plane(0, dy) for dy in range(1, Y)]
    peers = [sister, at_z(1), at_z(-1), at_z(half)] + x_near + y_near

    def tell(which, whom):
        for peer in whom:
            pl.semaphore_signal(known.at[which], inc=1, device_id=peer, device_id_type=pl.DeviceIdType.MESH)

    for peer in peers:
        pl.semaphore_signal(barrier, inc=1, device_id=peer, device_id_type=pl.DeviceIdType.MESH)
    pl.semaphore_wait(barrier, len(peers))
    for copy in swap:
        copy.start()

    size = held // SUBS
    odd = lax.rem(x + y, 2)

    def piece(slot, sub):
        part = lax.rem(sub // (SUBS // 2) + core, 2)
        start = part * held + odd * (held // 2) + sub % (SUBS // 2) * size
        return cg.at[pl.ds(lax.rem(slot + Z, Z) * per + start, size)]

    def beside(sub):
        step = (1 - 2 * odd) * (1 - 2 * (sub // 2))
        return at_plane(step + X, 0) if sub % 2 == 0 else at_plane(0, step + Y)

    started = []

    def go(copies):
        for copy in copies:
            copy.start()
        started.extend(copies)
        return copies

    def share(step, sub):
        slots = [z - step, z + step] if step < half else [z + step]
        refs = [piece(slot, sub) for slot in slots]
        return go([
            remote(ref, ref, side_send.at[i, step - 1, sub], side_recv.at[i, step - 1, sub], beside(sub))
            for i, ref in enumerate(refs)
        ])

    def hop(step, sub):
        refs = [piece(z - (step - 1), sub), piece(z + (step - 1), sub)]
        return go([
            remote(ref, ref, ring_send.at[i, step - 1, sub], ring_recv.at[i, step - 1, sub], at_z(1 - 2 * i))
            for i, ref in enumerate(refs)
        ])

    def fourth(slot):
        at = y // 2
        start = at // 2 * held + odd * (held // 2) + at % 2 * 2
        return cg.at[pl.ds(lax.rem(slot + Z, Z) * per + start, 2)]

    chains = []
    for copy in local:
        copy.wait()
    for sub in range(SUBS // 2):
        chains.append([hop(1, sub)])
    for copy in swap:
        copy.wait_recv()
    far = remote(fourth(z), fourth(z), far_send.at[0], far_recv.at[0], at_z(half))
    far.start()
    for sub in range(SUBS // 2, SUBS):
        chains.append([hop(1, sub)])

    lane = lax.broadcasted_iota(jnp.int32, (8, 128), 1)
    listed = jnp.zeros((8, 128), jnp.int32)
    for copy in lists:
        copy.wait()
    for t in range(16):
        listed = jnp.where(lane == t, owner_ref[t] * held + block_ref[t], listed)
    idx_v[0] = listed
    idx_copy = remote(idx_v.at[0], idx_v.at[1], idx_send, idx_recv, sister)
    idx_copy.start()
    tell(0, y_near)
    tell(1, x_near)

    rows = lax.broadcasted_iota(jnp.int32, (768, 768), 0)
    want = (rows & 15) * BS + (rows >> 4)
    perm[...] = (lax.broadcasted_iota(jnp.int32, (768, 768), 1) == want).astype(jnp.bfloat16)

    def turn(part):
        rhs = tiles[:, :, part * 768:(part + 1) * 768].reshape(768, 768)

        def body(i, carry):
            start = pl.multiple_of(i * 256, 256)
            got = dot(perm[pl.ds(start, 256), :], rhs, NT).astype(jnp.bfloat16)
            tt[core, pl.ds(i * 16, 16), part * 16:(part + 1) * 16, :] = got.reshape(16, 16, 768)
            return carry

        lax.fori_loop(0, 3, body, 0)

    turned = []

    def turn_next():
        part = len(turned)
        turn(part)
        ref = tt.at[core, :, part * 16:(part + 1) * 16]
        turned.append(remote(ref, ref, tt_send.at[part], tt_recv.at[part], sister))
        turned[-1].start()

    sides, rounds = [], []
    pl.semaphore_wait(known.at[0], 2)
    tell(2, y_next)
    tile_copy.wait()
    turn_next()
    for step in range(2, half):
        for sub in range(SUBS):
            for copy in chains[sub][-1]:
                copy.wait_recv()
            chains[sub].append(hop(step, sub))
            sides += share(step - 1, sub)
        if step == 2:
            far.wait_recv()
            pl.semaphore_wait(known.at[2], 2)
            ref = fourth(z + half)
            for dy in (4, 2, 6):
                rounds.append(remote(ref, ref, far_send.at[dy], far_recv.at[dy], at_plane(0, dy)))
                rounds[-1].start()
            pl.semaphore_wait(known.at[1], 2)
            tell(3, y_ring)
        turn_next()
    idx_copy.wait_recv()
    fetch = pltpu.make_async_copy(idx_v.at[1], idx_s, idx_sem)
    fetch.start()
    for copy in rounds:
        copy.wait_recv()
    for sub in range(SUBS):
        sides += share(half, sub)
    for sub in range(SUBS):
        for copy in chains[sub][-1]:
            copy.wait_recv()
        sides += share(half - 1, sub)
    fetch.wait()
    for copy in turned:
        copy.wait_recv()
    for copy in sides:
        copy.wait_recv()

    for t in range(16):
        picked[core, t * BS:(t + 1) * BS, :] = cg[owner_ref[t] * held + block_ref[t]]
        picked[other, t * BS:(t + 1) * BS, :] = cg[idx_s[0, t]]

    halos = []
    for b in range(BS // PB):
        ps = pl.ds(b * PB, PB)
        for r in range(2):
            right = picked[r]

            got = dot(tt[r, ps].reshape(PB * BS, 768), right, NN).astype(jnp.bfloat16)
            got = got.reshape(PB, BS, 256)
            occ[ps, r * BS:(r + 1) * BS, :] = got[:, :, :128]
            rsp[ps, r * BS:(r + 1) * BS, :] = got[:, :, 128:]
        down = remote(rsp.at[ps, 0:HW], halo.at[1, ps], halo_send.at[1, b], halo_recv.at[1, b], at_z(-1))
        up = remote(rsp.at[ps, 2 * BS - HW:2 * BS], halo.at[0, ps], halo_send.at[0, b], halo_recv.at[0, b], at_z(1))
        down.start()
        up.start()
        halos += [(down, up)]

    total = jnp.zeros((2 * BS, 2 * BS + 2 * HW), jnp.float32)
    for b in range(BS // PB):
        for copy in halos[b]:
            copy.wait_recv()
        left, wide = [], []
        for p in range(b * PB, (b + 1) * PB):
            left.append(occ[p])
            wide.append(jnp.concatenate([halo[0, p], rsp[p], halo[1, p]], axis=0))
        total = total + dot(jnp.concatenate(left, axis=1), jnp.concatenate(wide, axis=1), NT)

    shape = (2 * BS, 2 * BS + 2 * HW)
    at_row, at_col = lax.broadcasted_iota(jnp.int32, shape, 0), lax.broadcasted_iota(jnp.int32, shape, 1)
    outside = jnp.logical_or(
        jnp.logical_and(z == 0, at_col < HW), jnp.logical_and(z == Z - 1, at_col >= 2 * BS + HW)
    )
    band[...] = jnp.where(outside, 0.0, total)

    for xx in range(X):
        for c in range(2):
            first = c * BS + 3 * (xx // 2)
            shift = BS * c
            if xx % 2 == 0:
                one, two = band[pl.ds(first, 8, stride=6), :], band[pl.ds(first + 1, 8, stride=6), :]
                a, b, cut = (128 - shift) % 128, (80 - shift) % 128, 80
            else:
                one, two = band[pl.ds(first + 1, 8, stride=6), :], band[pl.ds(first + 2, 8, stride=6), :]
                a, b, cut = (128 - shift - 40) % 128, (40 - shift) % 128, 40
            one = pltpu.roll(one, a, 1) if a else one
            two = pltpu.roll(two, b, 1) if b else two
            parts[c, xx] = jnp.where(lane < cut, one, two)

    cross = remote(parts.at[other], cross_in, s1_send, s1_recv, sister)
    cross.start()
    cross.wait_recv()
    pl.semaphore_wait(known.at[3], Y - 1)
    rows_out[...] = (parts[core] + cross_in[...]).reshape(X * Y, 1, 128)
    copies = []
    for i, (dx, dy) in enumerate(plane):
        there = lax.rem(x + dx, X) * Y + lax.rem(y + dy, Y)
        copies.append(remote(rows_out.at[there], rows_in.at[i], s2_send.at[i], s2_recv.at[i], at_plane(dx, dy)))
        copies[-1].start()
    rows_in[X * Y - 1] = rows_out[x * Y + y]
    for copy in copies:
        copy.wait_recv()
    out_ref[...] = jnp.sum(rows_in[...], axis=0) * factor
    for pair in halos:
        copies += pair
    for copy in swap + turned + started + rounds + copies + [idx_copy, far, cross]:
        copy.wait_send()


def local(tile_values, tile_owner, tile_block, coefficients):
    n_aux, n_ao = lax.axis_size("aux"), lax.axis_size("ao")
    Y, Z = n_aux // X, n_ao // 2
    count = tile_values.shape[0]
    held = coefficients.shape[0]
    factor = 1.0 / math.sqrt(256 * BS * n_aux)
    bf, f32 = jnp.bfloat16, jnp.float32
    dma = pltpu.SemaphoreType.DMA
    got = pl.pallas_call(
        functools.partial(kernel, Y, Z, factor),
        out_shape=jax.ShapeDtypeStruct((1, 128), f32),
        in_specs=[
            pl.BlockSpec(memory_space=pltpu.HBM),
            pl.BlockSpec(memory_space=pltpu.HBM),
            pl.BlockSpec(memory_space=pltpu.HBM),
            pl.BlockSpec(memory_space=pltpu.HBM),
        ],
        out_specs=pl.BlockSpec(memory_space=pltpu.VMEM),
        scratch_shapes=[
            pltpu.SMEM((count,), jnp.int32),
            pltpu.SMEM((count,), jnp.int32),
            pltpu.VMEM((count, BS, BS * BS), bf),
            pltpu.VMEM((768, 768), bf),
            pltpu.VMEM((2, BS, BS, 768), bf),
            pltpu.VMEM((n_ao * held, BS, 256), bf),
            pltpu.VMEM((2, 768, 256), bf),
            pltpu.VMEM((BS, 2 * BS, 128), bf),
            pltpu.VMEM((BS, 2 * BS, 128), bf),
            pltpu.VMEM((2, BS, HW, 128), bf),
            pltpu.VMEM((2 * BS, 2 * BS + 2 * HW), f32),
            pltpu.VMEM((2, X, 8, 128), f32),
            pltpu.VMEM((X, 8, 128), f32),
            pltpu.VMEM((X * Y, 1, 128), f32),
            pltpu.VMEM((X * Y, 1, 128), f32),
            pltpu.VMEM((2, 8, 128), jnp.int32),
            pltpu.SMEM((8, 128), jnp.int32),
            dma((2,)), dma, dma((2,)), dma((2,)), dma((2,)),
            dma((2, Z // 2, SUBS)), dma((2, Z // 2, SUBS)), dma((2, Z // 2, SUBS)), dma((2, Z // 2, SUBS)), dma((Y,)), dma((Y,)), dma((3,)), dma((3,)),
            dma, dma, dma,
            dma((2, BS // PB)), dma((2, BS // PB)),
            dma, dma, dma((X * Y,)), dma((X * Y,)),
            pltpu.SemaphoreType.REGULAR((4,)),
        ],
        compiler_params=pltpu.CompilerParams(
            collective_id=0, has_side_effects=True, vmem_limit_bytes=60 * 1024 * 1024
        ),
        name="exchange",
    )(tile_owner.reshape(count), tile_block, tile_values, coefficients)
    return got[:, :BS * (BS + 2 * HW) // n_aux]


def solution(mesh):
    placed = (
        P(("aux", "ao"), None, None),
        P(("aux", "ao"), None),
        P(("aux", "ao")),
        P("ao", None, None),
    )
    return jax.shard_map(
        local, mesh=mesh, in_specs=placed, out_specs=P("ao", "aux"), check_vma=False
    )
```
